1024 devices in a mesh: section: 16 (over z_hi, x), dp: 64 (over z_lo, y, core).
Axes of the slice: x: 4, y: 8, z: 16 (z_hi: 4, z_lo: 4; z = z_hi * 4 + z_lo), core: 2. Of those that a mesh axis runs over, the one named last changes fastest.
Arguments:
- fresh_q: bfloat16 [16, 7168, 2048], P('section', 'dp'), may hold values from -6 to 6
- current_key_value: bfloat16 [16, 7168, 512], P('section', 'dp'), may hold values from -6 to 6
- held_q: bfloat16 [16, 7168, 2048], P('section', 'dp'), may hold values from -6 to 6
- retained_key_value: bfloat16 [16, 7168, 512], P('section', 'dp'), may hold values from -6 to 6
- cotangent: bfloat16 [16, 7168, 2048], P('section', 'dp'), may hold values from -6 to 6
- norm_gains: float32 [16, 2, 128], P('section'), may hold values from 0.5 to 1.5
- plan: int32 [16, 2], P('section'), may hold values from 0 to 15, as said below
- segment_ids: int32 [64, 16, 112], P('dp'), may hold values from 0 to 3, never falling along the last dimension, each value on 1 to 56 neighbouring positions
Outputs:
- attention_out: bfloat16 [16, 7168, 2048], P('section', 'dp')
- stored_q: bfloat16 [16, 7168, 2048], P('section', 'dp')
- stored_kv: bfloat16 [16, 7168, 512], P('section', 'dp')
- grad_q: bfloat16 [16, 7168, 2048], P('section', 'dp')
- key_value_gradient: bfloat16 [16, 7168, 512], P('section', 'dp')
- gain_grads: float32 [16, 2, 128], P('section')
The draws below stay inside these ranges and needn't reach their ends.
Inputs may be any that keep to these rules, and one draw needn't show every extreme that they name: `plan`: each of the two columns holds every microbatch number 0 to 15 exactly once.
All inputs are finite; a program needn't handle non-finite values.
Results may differ from the reference program's by a relative error of at most 0.0065.
Values may be sent and summed in bfloat16 or wider, within the bound.
A program may use at most 32 MiB of HBM per device.

```python
import math
import jax
import jax.numpy as jnp
import numpy as np
from jax import lax

MB = 112
HQ = 16
KV_HEAD_COUNT = 2
HEAD_SIZE = 128
QUERY_PER_KV = 8
RELAY_SECTIONS = 16
REPLICAS = 64
MICRO = 16
SECTION_TOKENS = 7168
N_DP = 64


def draw_plan(key, part):
    forward_ids = jax.random.permutation(jax.random.fold_in(key, 11), MICRO)
    backward_ids = jax.random.permutation(jax.random.fold_in(key, 23), MICRO)
    return jnp.stack([forward_ids, backward_ids], axis=1).astype(jnp.int32)


def steps_of(stream_key, dims, pieces, least, largest):
    def one(axis_at, shards_of):
        heights = jax.random.uniform(jax.random.fold_in(jax.random.fold_in(stream_key, 6), axis_at), (shards_of,), jnp.float32, least / len(pieces), largest / len(pieces))
        return jnp.repeat(jnp.exp(heights), dims[axis_at] // shards_of).reshape((-1,) + (1,) * (len(dims) - axis_at - 1))

    level = one(*pieces[0])
    for cut in pieces[1:]:
        level = level * one(*cut)
    return level


def split_up(amount, total, bound, lean):
    loads = [(1 << 20) // math.isqrt(grade ** lean) + 1 for grade in range(2, amount + 1)]
    rest, given = total - bound - (amount - 1), [1] * (amount - 1)
    while rest > 0:
        candidates = [i for i in range(amount - 1) if given[i] < bound]
        mass, remaining = sum([loads[i] for i in candidates]), rest
        for i in candidates:
            extra = min(bound - given[i], max(1, remaining * loads[i] // mass), rest)
            given[i] = given[i] + extra
            rest = rest - extra
    return np.array([bound] + given)


def uneven_parts(own_key, number_of, total, bound, skew):
    if number_of == 2:
        one = jax.random.randint(own_key, (), max(1, total - bound), min(bound, total - 1) + 1)
        return jnp.stack([one, total - one])
    sizes = jnp.asarray(split_up(number_of, total, bound, skew), jnp.int32)
    couples = (number_of - 1) // 2
    source_of, receiver = sizes[1:1 + 2 * couples:2], sizes[2:2 + 2 * couples:2]
    slack = jnp.minimum(source_of - 1, bound - receiver)
    passed = jax.random.randint(jax.random.fold_in(own_key, 1), (couples,), 0, 1 << 20) % (slack + 1)
    sizes = sizes.at[1:1 + 2 * couples:2].set(source_of - passed).at[2:2 + 2 * couples:2].set(receiver + passed)
    return sizes[jax.random.permutation(jax.random.fold_in(own_key, 2), number_of)]


def normal_values(rng, extent, spread, bound, shards=(), kind=jnp.bfloat16):
    entries = jax.random.normal(rng, extent, jnp.float32) * spread
    if len(shards) > 0:
        entries = steps_of(rng, extent, shards, -0.22, 0.18) * entries
    return jnp.clip(entries, min=-bound, max=bound).astype(kind)


def setup_inputs(seed: int = 0) -> dict:
    seeds = jax.random.split(jax.random.key(seed), 9)
    fresh_q = normal_values(seeds[0], (RELAY_SECTIONS, SECTION_TOKENS, HQ * HEAD_SIZE), 1.0, 6.0, ((0, 16), (1, 64)))
    current_key_value = normal_values(seeds[1], (RELAY_SECTIONS, SECTION_TOKENS, 2 * KV_HEAD_COUNT * HEAD_SIZE), 1.0, 6.0, ((0, 16), (1, 64)))
    held_q = normal_values(seeds[2], (RELAY_SECTIONS, SECTION_TOKENS, HQ * HEAD_SIZE), 1.0, 6.0, ((0, 16), (1, 64)))
    retained_key_value = normal_values(seeds[3], (RELAY_SECTIONS, SECTION_TOKENS, 2 * KV_HEAD_COUNT * HEAD_SIZE), 1.0, 6.0, ((0, 16), (1, 64)))
    cotangent = normal_values(seeds[4], (RELAY_SECTIONS, SECTION_TOKENS, HQ * HEAD_SIZE), 1.0, 6.0, ((0, 16), (1, 64)))
    norm_gains = jnp.clip(1.0 + 0.1 * jax.random.normal(seeds[5], (RELAY_SECTIONS, 2, HEAD_SIZE), jnp.float32), 0.5, 1.5)
    plan = draw_plan(jax.random.fold_in(seeds[8], 71), 0)
    segment_ids = jax.vmap(lambda own: jnp.searchsorted(jnp.cumsum(uneven_parts(own, 4, MB, MB // 2, 2)), jnp.arange(MB), side="right"))(jax.random.split(seeds[7], REPLICAS * MICRO)).reshape((REPLICAS, MICRO, MB)).astype(jnp.int32)
    return {"fresh_q": fresh_q, "current_key_value": current_key_value, "held_q": held_q, "retained_key_value": retained_key_value, "cotangent": cotangent, "norm_gains": norm_gains, "plan": plan, "segment_ids": segment_ids}


EPSILON = 1e-06

def rounded_values(values):
    return lax.optimization_barrier(values.astype(jnp.bfloat16)).astype(jnp.float32)

def allowed_pairs(segment_row):
    row_sum_total = segment_row.shape[0]
    rows_at = jnp.arange(row_sum_total)[:, None]
    cols_at = jnp.arange(row_sum_total)[None, :]
    return (cols_at <= rows_at) & (segment_row[:, None] == segment_row[None, :])

def apply_norm(values, gain, heads):
    row_sum_total = values.shape[0]
    widened = values.astype(jnp.float32).reshape(row_sum_total, heads, HEAD_SIZE)
    factor = lax.rsqrt(lax.optimization_barrier(jnp.mean(widened * widened, axis=-1, keepdims=True)) + EPSILON)
    return (widened, factor, widened * factor * gain)

def attention_probs(query_rows, key_value_pair, gain_per_row, segment_row):
    row_sum_total = query_rows.shape[0]
    q_wide, q_factor, normalized_query = apply_norm(query_rows, gain_per_row[0], HQ)
    expanded_key, key_factor, normalized_key = apply_norm(key_value_pair[:, :KV_HEAD_COUNT * HEAD_SIZE], gain_per_row[1], KV_HEAD_COUNT)
    query_converted = rounded_values(normalized_query).reshape(row_sum_total, KV_HEAD_COUNT, QUERY_PER_KV, HEAD_SIZE)
    k_cast = rounded_values(normalized_key)
    scores = jnp.einsum('qhgd,khd->hgqk', query_converted, k_cast) * (1.0 / math.sqrt(HEAD_SIZE))
    weights = jnp.where(allowed_pairs(segment_row), jnp.exp(scores), 0.0)
    attn_probs = weights / lax.optimization_barrier(jnp.sum(weights, axis=-1, keepdims=True))
    return (q_wide, q_factor, query_converted, expanded_key, key_factor, k_cast, attn_probs)

def forward(query_rows, key_value_pair, gain_per_row, segment_row):
    row_sum_total = query_rows.shape[0]
    attn_probs = attention_probs(query_rows, key_value_pair, gain_per_row, segment_row)[6]
    value_portion = key_value_pair[:, KV_HEAD_COUNT * HEAD_SIZE:].astype(jnp.float32).reshape(row_sum_total, KV_HEAD_COUNT, HEAD_SIZE)
    output = jnp.einsum('hgqk,khd->qhgd', rounded_values(attn_probs), value_portion)
    return output.reshape(row_sum_total, HQ * HEAD_SIZE).astype(jnp.bfloat16)

def norm_back(widened, factor, gain, d_normed):
    scaled = gain * d_normed
    inner = lax.optimization_barrier(jnp.sum(widened * scaled, axis=-1, keepdims=True)) / HEAD_SIZE
    d_input = factor * scaled - widened * factor * factor * factor * inner
    d_gain = lax.optimization_barrier(jnp.sum(d_normed * widened * factor, axis=(0, 1)))
    return (d_input, d_gain)

def backward(query_rows, key_value_pair, gain_per_row, segment_row, received_payload):
    row_sum_total = query_rows.shape[0]
    q_wide, q_factor, query_converted, expanded_key, key_factor, k_cast, attn_probs = attention_probs(query_rows, key_value_pair, gain_per_row, segment_row)
    value_portion = key_value_pair[:, KV_HEAD_COUNT * HEAD_SIZE:].astype(jnp.float32).reshape(row_sum_total, KV_HEAD_COUNT, HEAD_SIZE)
    expanded_heads = received_payload.astype(jnp.float32).reshape(row_sum_total, KV_HEAD_COUNT, QUERY_PER_KV, HEAD_SIZE)
    prob_cast = rounded_values(attn_probs)
    d_probs = jnp.einsum('qhgd,khd->hgqk', expanded_heads, value_portion)
    value_gradient = jnp.einsum('hgqk,qhgd->khd', prob_cast, expanded_heads)
    centre = lax.optimization_barrier(jnp.sum(attn_probs * d_probs, axis=-1, keepdims=True))
    d_scores = rounded_values(attn_probs * (d_probs - centre))
    score_scale = 1.0 / math.sqrt(HEAD_SIZE)
    d_qn = jnp.einsum('hgqk,khd->qhgd', d_scores, k_cast).reshape(row_sum_total, HQ, HEAD_SIZE) * score_scale
    d_kn = jnp.einsum('hgqk,qhgd->khd', d_scores, query_converted) * score_scale
    grad_query, q_gain = norm_back(q_wide, q_factor, gain_per_row[0], d_qn)
    key_gradient, k_gain = norm_back(expanded_key, key_factor, gain_per_row[1], d_kn)
    grad_q = grad_query.reshape(row_sum_total, HQ * HEAD_SIZE).astype(jnp.bfloat16)
    key_value_gradient = jnp.concatenate([key_gradient.reshape(row_sum_total, KV_HEAD_COUNT * HEAD_SIZE), value_gradient.reshape(row_sum_total, KV_HEAD_COUNT * HEAD_SIZE)], axis=1).astype(jnp.bfloat16)
    return (grad_q, key_value_gradient, jnp.stack([q_gain, k_gain]))

def reference(fresh_q, current_key_value, held_q, retained_key_value, cotangent, norm_gains, plan, segment_ids):
    section_total = fresh_q.shape[0]

    def split_rows(values):
        return values.reshape(section_total, N_DP, MB, values.shape[-1])
    fetched_q = split_rows(held_q[::-1])
    fetched_kv = split_rows(retained_key_value[::-1])
    upstream = split_rows(jnp.roll(cotangent, -1, axis=0))

    def per_section(inputs):
        query_rows, key_value_pair, old_query, old_keyval, received_payload, gain_per_row, id_table = inputs
        forward_ids = segment_ids[:, id_table[0], :]
        backward_ids = segment_ids[:, id_table[1], :]
        outputs = jax.vmap(forward, in_axes=(0, 0, None, 0))(query_rows, key_value_pair, gain_per_row, forward_ids)
        grad_q, key_value_gradient, gain_terms = jax.vmap(backward, in_axes=(0, 0, None, 0, 0))(old_query, old_keyval, gain_per_row, backward_ids, received_payload)
        return (outputs, grad_q, key_value_gradient, lax.optimization_barrier(jnp.sum(gain_terms, axis=0)) / N_DP)
    outputs, grad_q, key_value_gradient, gain_grads = lax.map(per_section, (split_rows(fresh_q), split_rows(current_key_value), fetched_q, fetched_kv, upstream, norm_gains, plan))
    attention_out = jnp.roll(outputs, 1, axis=0).reshape(fresh_q.shape)
    return (attention_out, fresh_q[::-1], current_key_value[::-1], grad_q.reshape(held_q.shape), key_value_gradient.reshape(retained_key_value.shape), gain_grads)
```

```python
import math

import jax
import jax.numpy as jnp
from jax import lax
from jax.sharding import PartitionSpec as P

HQ = 16
KV_HEAD_COUNT = 2
HEAD_SIZE = 128
QUERY_PER_KV = 8


EPSILON = 1e-06


def mirrored(value, axis):
    last = lax.axis_size(axis) - 1
    return lax.ppermute(value, axis, [(source, last - source) for source in range(last + 1)])


def shifted(block, axis, distance):
    devices = range(lax.axis_size(axis))
    route = [((i - distance) % len(devices), i) for i in devices]
    return lax.ppermute(block, axis, route)


def allowed_pairs(segment_row):
    row_sum_total = segment_row.shape[0]
    rows_at = jnp.arange(row_sum_total)[:, None]
    cols_at = jnp.arange(row_sum_total)[None, :]
    return (cols_at <= rows_at) & (segment_row[:, None] == segment_row[None, :])


def apply_norm(values, gain, heads):
    row_sum_total = values.shape[0]
    widened = values.astype(jnp.float32).reshape(row_sum_total, heads, HEAD_SIZE)
    factor = lax.rsqrt(jnp.mean(widened * widened, axis=-1, keepdims=True) + EPSILON)
    return (widened, factor, widened * factor * gain)


def attention_probs(query_rows, key_value_pair, gain_per_row, segment_row):
    row_sum_total = query_rows.shape[0]
    q_wide, q_factor, normalized_query = apply_norm(query_rows, gain_per_row[0], HQ)
    expanded_key, key_factor, normalized_key = apply_norm(
        key_value_pair[:, : KV_HEAD_COUNT * HEAD_SIZE], gain_per_row[1], KV_HEAD_COUNT
    )
    query_converted = normalized_query.astype(jnp.bfloat16).reshape(
        row_sum_total, KV_HEAD_COUNT, QUERY_PER_KV, HEAD_SIZE
    )
    k_cast = normalized_key.astype(jnp.bfloat16)
    scores = jnp.einsum(
        "qhgd,khd->hgqk", query_converted, k_cast, preferred_element_type=jnp.float32
    ) * (1.0 / math.sqrt(HEAD_SIZE))
    weights = jnp.where(allowed_pairs(segment_row), jnp.exp(scores), 0.0)
    attn_probs = weights / jnp.sum(weights, axis=-1, keepdims=True)
    return (q_wide, q_factor, query_converted, expanded_key, key_factor, k_cast, attn_probs)


def forward(query_rows, key_value_pair, gain_per_row, segment_row):
    row_sum_total = query_rows.shape[0]
    attn_probs = attention_probs(query_rows, key_value_pair, gain_per_row, segment_row)[6]
    value_portion = key_value_pair[:, KV_HEAD_COUNT * HEAD_SIZE :].reshape(
        row_sum_total, KV_HEAD_COUNT, HEAD_SIZE
    )
    output = jnp.einsum(
        "hgqk,khd->qhgd",
        attn_probs.astype(jnp.bfloat16),
        value_portion,
        preferred_element_type=jnp.float32,
    )
    return output.reshape(row_sum_total, HQ * HEAD_SIZE).astype(jnp.bfloat16)


def norm_back(widened, factor, gain, d_normed):
    scaled = gain * d_normed
    inner = jnp.sum(widened * scaled, axis=-1, keepdims=True) / HEAD_SIZE
    d_input = factor * scaled - widened * factor * factor * factor * inner
    d_gain = jnp.sum(d_normed * widened * factor, axis=(0, 1))
    return (d_input, d_gain)


def backward(query_rows, key_value_pair, gain_per_row, segment_row, received_payload):
    row_sum_total = query_rows.shape[0]
    q_wide, q_factor, query_converted, expanded_key, key_factor, k_cast, attn_probs = (
        attention_probs(query_rows, key_value_pair, gain_per_row, segment_row)
    )
    value_portion = key_value_pair[:, KV_HEAD_COUNT * HEAD_SIZE :].reshape(
        row_sum_total, KV_HEAD_COUNT, HEAD_SIZE
    )
    expanded_heads = received_payload.reshape(row_sum_total, KV_HEAD_COUNT, QUERY_PER_KV, HEAD_SIZE)
    prob_cast = attn_probs.astype(jnp.bfloat16)
    d_probs = jnp.einsum(
        "qhgd,khd->hgqk", expanded_heads, value_portion, preferred_element_type=jnp.float32
    )
    value_gradient = jnp.einsum(
        "hgqk,qhgd->khd", prob_cast, expanded_heads, preferred_element_type=jnp.float32
    )
    centre = jnp.sum(attn_probs * d_probs, axis=-1, keepdims=True)
    d_scores = (attn_probs * (d_probs - centre)).astype(jnp.bfloat16)
    score_scale = 1.0 / math.sqrt(HEAD_SIZE)
    d_qn = (
        jnp.einsum("hgqk,khd->qhgd", d_scores, k_cast, preferred_element_type=jnp.float32).reshape(
            row_sum_total, HQ, HEAD_SIZE
        )
        * score_scale
    )
    d_kn = (
        jnp.einsum("hgqk,qhgd->khd", d_scores, query_converted, preferred_element_type=jnp.float32)
        * score_scale
    )
    grad_query, q_gain = norm_back(q_wide, q_factor, gain_per_row[0], d_qn)
    key_gradient, k_gain = norm_back(expanded_key, key_factor, gain_per_row[1], d_kn)
    grad_q = grad_query.reshape(row_sum_total, HQ * HEAD_SIZE).astype(jnp.bfloat16)
    key_value_gradient = jnp.concatenate(
        [
            key_gradient.reshape(row_sum_total, KV_HEAD_COUNT * HEAD_SIZE),
            value_gradient.reshape(row_sum_total, KV_HEAD_COUNT * HEAD_SIZE),
        ],
        axis=1,
    ).astype(jnp.bfloat16)
    return (grad_q, key_value_gradient, jnp.stack([q_gain, k_gain]))


def local(
    fresh_q, current_key_value, held_q, retained_key_value, cotangent, norm_gains, plan, segment_ids
):
    gain_per_row = norm_gains[0]
    id_table = segment_ids[0]
    forward_ids = lax.dynamic_index_in_dim(id_table, plan[0, 0], 0, keepdims=False)
    backward_ids = lax.dynamic_index_in_dim(id_table, plan[0, 1], 0, keepdims=False)
    arrived = mirrored((fresh_q, current_key_value, held_q, retained_key_value), "section")
    forward_out = forward(fresh_q[0], current_key_value[0], gain_per_row, forward_ids)
    attention_out = shifted(forward_out[None], "section", 1)
    upstream = shifted(cotangent, "section", -1)
    grad_q, key_value_gradient, gain_terms = backward(
        arrived[2][0], arrived[3][0], gain_per_row, backward_ids, upstream[0]
    )
    gain_total = lax.psum(gain_terms, "dp") / lax.axis_size("dp")
    return (
        attention_out,
        arrived[0],
        arrived[1],
        grad_q[None],
        key_value_gradient[None],
        gain_total[None],
    )


def solution(mesh):
    placed = (
        P("section", "dp", None),
        P("section", "dp", None),
        P("section", "dp", None),
        P("section", "dp", None),
        P("section", "dp", None),
        P("section", None, None),
        P("section", None),
        P("dp", None, None),
    )
    return jax.shard_map(
        local,
        mesh=mesh,
        in_specs=placed,
        out_specs=(
            P("section", "dp", None),
            P("section", "dp", None),
            P("section", "dp", None),
            P("section", "dp", None),
            P("section", "dp", None),
            P("section", None, None),
        ),
        check_vma=False,
    )
```

```python
import functools
import math

import jax
import jax.numpy as jnp
from jax import lax
from jax.experimental import pallas as pl
from jax.experimental.pallas import tpu as pltpu
from jax.sharding import PartitionSpec as P

F32, BF16 = jnp.float32, jnp.bfloat16
D = 128
HEADS, KV_HEADS = 16, 2
PER_KV = HEADS // KV_HEADS
GROUP = 4
EPSILON = 1e-06
SCALE = 1.0 / math.sqrt(D)
MESH = pl.DeviceIdType.MESH

HELD_KV, HELD_Q, COT, ATT, SIDE, GRAD_Q, GRAD_KV, GAIN, FRESH_KV, FRESH_Q = range(10)
CHUNKS = HEADS // GROUP
ROUND = FRESH_Q + CHUNKS

L_FQ, L_FKV, L_SIDE, L_HQ, L_HKV, L_COT, L_GQ, L_GKV, L_GAIN, L_ATT, L_CHUNK = range(11)


def dot(a, b, dims):
    return lax.dot_general(a, b, ((dims[:1], dims[1:]), ((), ())), preferred_element_type=F32)


def lane_sum(a):
    return jnp.sum(a, axis=-1, keepdims=True)


def fold(a):
    return jnp.sum(a.reshape(-1, 8, D), axis=0)


def head(i):
    start = i * D
    return pl.ds(start if isinstance(i, int) else pl.multiple_of(start, D), D)


def prepare(kv, side, slot, row, keys, values, mask):
    tokens = kv.shape[0]
    ids = jnp.broadcast_to(side[slot, row : row + 1, :], (D, D))
    rows = lax.broadcasted_iota(jnp.int32, (D, D), 0)
    cols = lax.broadcasted_iota(jnp.int32, (D, D), 1)
    allowed = jnp.where((ids == ids.T) & (cols <= rows), 1.0, 0.0)
    mask[...] = allowed[:tokens]
    gain = side[slot, 1:2, :]
    pad = jnp.zeros((D - tokens, D), BF16)
    for g in range(KV_HEADS):
        x = kv[:, head(g)].astype(F32)
        r = lax.rsqrt(jnp.mean(x * x, axis=-1, keepdims=True) + EPSILON)
        keys[g, :tokens, :] = (x * r * gain).astype(BF16)
        keys[g, tokens:, :] = pad
        values[g, :tokens, :] = kv[:, head(KV_HEADS + g)]
        values[g, tokens:, :] = pad


def probabilities(q, lanes, gain, k, mask):
    x = q[:, lanes].astype(F32)
    r = lax.rsqrt(jnp.mean(x * x, axis=-1, keepdims=True) + EPSILON)
    qn = (x * r * gain).astype(BF16)
    w = jnp.exp(dot(qn, k, (1, 1)) * SCALE) * mask[...]
    return x, r, qn, w * (1.0 / lane_sum(w))


def forward_step(it, q, side, slot, keys, values, mask, out):
    g = it // (PER_KV // GROUP)
    k, v = keys[g], values[g]
    gain = side[slot, 0:1, :]
    for u in range(GROUP):
        lanes = head(it * GROUP + u)
        p = probabilities(q, lanes, gain, k, mask)[3]
        out[:, lanes] = dot(p.astype(BF16), v, (1, 0)).astype(BF16)


def backward(q, kv, cot, side, slot, keys, values, mask, dk, dv, sums, grad_q, grad_kv):
    tokens = q.shape[0]
    prepare(kv, side, slot, 3, keys, values, mask)
    dk[...] = jnp.zeros_like(dk)
    dv[...] = jnp.zeros_like(dv)
    sums[...] = jnp.zeros_like(sums)

    @pl.loop(0, CHUNKS)
    def _(it):
        g = it // (PER_KV // GROUP)
        k, v = keys[g], values[g]
        gain = side[slot, 0:1, :]
        for u in range(GROUP):
            lanes = head(it * GROUP + u)
            x, r, qn, p = probabilities(q, lanes, gain, k, mask)
            up = cot[:, lanes]
            d_p = dot(up, v, (1, 1))
            dv[g] += dot(p.astype(BF16), up, (0, 0))
            d_s = (p * (d_p - lane_sum(p * d_p))).astype(BF16)
            d_qn = dot(d_s, k, (1, 0)) * SCALE
            dk[g] += dot(d_s, qn, (0, 0))
            scaled = gain * d_qn
            inner = lane_sum(x * scaled) * (1.0 / D)
            grad_q[:, lanes] = (r * scaled - x * (r * r * r * inner)).astype(BF16)
            sums[0] += fold(d_qn * x * r)

    gain = side[slot, 1:2, :]
    for g in range(KV_HEADS):
        x = kv[:, head(g)].astype(F32)
        r = lax.rsqrt(jnp.mean(x * x, axis=-1, keepdims=True) + EPSILON)
        d_kn = dk[g, :tokens, :] * SCALE
        scaled = gain * d_kn
        inner = lane_sum(x * scaled) * (1.0 / D)
        grad_kv[:, head(g)] = (r * scaled - x * (r * r * r * inner)).astype(BF16)
        grad_kv[:, head(KV_HEADS + g)] = dv[g, :tokens, :].astype(BF16)
        sums[1] += fold(d_kn * x * r)


def gain_rows(sums):
    q = jnp.sum(sums[0], axis=0, keepdims=True)
    k = jnp.sum(sums[1], axis=0, keepdims=True)
    row = lax.broadcasted_iota(jnp.int32, (8, D), 0)
    return jnp.where(row == 0, q, jnp.where(row == 1, k, 0.0))


def kernel(
    sections, replicas,
    fresh_q, fresh_kv, held_q, held_kv, cot, side,
    att_out, stored_q, stored_kv, grad_q_out, grad_kv_out, gain_out,
    q_vm, kv_vm, att_vm, hq_vm, hkv_vm, cot_vm, gq_vm, gkv_vm, side_vm,
    own_q, own_kv, own_cot, far_gq, far_gkv,
    keys, values, mask, dk, dv, sums, part, got, final,
    send, recv, local,
):
    s, d = lax.axis_index("section"), lax.axis_index("dp")
    mirror, up, down = sections - 1 - s, lax.rem(s + 1, sections), lax.rem(s + sections - 1, sections)
    rounds = replicas.bit_length() - 1
    partners = [d + (1 << i) * (1 - 2 * lax.rem(d // (1 << i), 2)) for i in range(rounds)]
    half = sections // 2
    giver = (s == half - 1) | (s == sections - 1)
    taker = (s == 0) | (s == half)
    normal = jnp.logical_not(giver | taker)

    def remote(src, dst, slot, section):
        return pltpu.make_async_remote_copy(
            src_ref=src, dst_ref=dst, send_sem=send.at[slot], recv_sem=recv.at[slot],
            device_id={"section": section}, device_id_type=MESH,
        )

    def chunk(ref, i):
        start = i * GROUP * D
        return ref.at[:, pl.ds(start if isinstance(i, int) else pl.multiple_of(start, GROUP * D), GROUP * D)]

    def load(src, dst, slot):
        return pltpu.make_async_copy(src, dst, local.at[slot])

    copy_held_kv = remote(held_kv.at[0], hkv_vm, HELD_KV, mirror)
    copy_held_q = remote(held_q.at[0], hq_vm, HELD_Q, mirror)
    copy_cot = remote(cot.at[0], cot_vm, COT, down)
    copy_att = remote(att_vm, att_out.at[0], ATT, up)
    copy_side = remote(side, side_vm.at[1], SIDE, mirror)
    copy_gq = remote(far_gq, grad_q_out.at[0], GRAD_Q, mirror)
    copy_gkv = remote(far_gkv, grad_kv_out.at[0], GRAD_KV, mirror)
    copy_gain = remote(final.at[1], gain_out, GAIN, mirror)
    copy_fresh_kv = remote(fresh_kv.at[0], stored_kv.at[0], FRESH_KV, mirror)

    def copy_fresh_q(i):
        return remote(chunk(fresh_q.at[0], i), chunk(stored_q.at[0], i), FRESH_Q + i, mirror)

    load_fq = load(fresh_q.at[0], q_vm, L_FQ)
    load_fkv = load(fresh_kv.at[0], kv_vm, L_FKV)
    load_side = load(side, side_vm.at[0], L_SIDE)
    load_hq = load(held_q.at[0], own_q, L_HQ)
    load_hkv = load(held_kv.at[0], own_kv, L_HKV)
    load_cot = load(cot.at[0], own_cot, L_COT)
    put_gq = load(gq_vm, grad_q_out.at[0], L_GQ)
    put_gkv = load(gkv_vm, grad_kv_out.at[0], L_GKV)
    put_gain = load(final.at[0], gain_out, L_GAIN)

    barrier = pltpu.get_barrier_semaphore()
    for section in (mirror, up, down):
        pl.semaphore_signal(barrier, inc=1, device_id={"section": section}, device_id_type=MESH)
    for partner in partners:
        pl.semaphore_signal(barrier, inc=1, device_id={"dp": partner}, device_id_type=MESH)

    load_side.start()

    @pl.when(jnp.logical_not(giver))
    def _():
        load_fkv.start()
        load_fq.start()

    @pl.when(taker)
    def _():
        load_hkv.start()
        load_hq.start()
        load_cot.start()

    pl.semaphore_wait(barrier, 3 + rounds)

    @pl.when(giver)
    def _():
        copy_side.start()

    @pl.when(jnp.logical_not(taker))
    def _():
        copy_cot.start()
        copy_held_kv.start()
        copy_held_q.start()

    @pl.when(jnp.logical_not(normal))
    def _():
        copy_fresh_kv.start()
        for i in range(CHUNKS):
            copy_fresh_q(i).start()

    load_side.wait()

    @pl.when(jnp.logical_not(giver))
    def _():
        load_fkv.wait()
        prepare(kv_vm, side_vm, 0, 2, keys, values, mask)
        load_fq.wait()

        @pl.loop(0, CHUNKS)
        def _(it):
            forward_step(it, q_vm, side_vm, 0, keys, values, mask, att_vm)

        copy_att.start()

    @pl.when(normal)
    def _():
        copy_fresh_kv.start()
        for i in range(CHUNKS):
            copy_fresh_q(i).start()

    @pl.when(taker)
    def _():
        load_hkv.wait()
        load_hq.wait()
        load_cot.wait()
        copy_side.wait_recv()
        backward(own_q, own_kv, own_cot, side_vm, 1, keys, values, mask, dk, dv, sums, far_gq, far_gkv)
        copy_gkv.start()
        copy_gq.start()
        part[0, 1] = gain_rows(sums)

    @pl.when(normal)
    def _():
        part[0, 1] = jnp.zeros((8, D), F32)

    @pl.when(jnp.logical_not(giver))
    def _():
        copy_cot.wait_recv()
        copy_held_kv.wait_recv()
        copy_held_q.wait_recv()
        backward(hq_vm, hkv_vm, cot_vm, side_vm, 0, keys, values, mask, dk, dv, sums, gq_vm, gkv_vm)
        put_gkv.start()
        put_gq.start()
        part[0, 0] = gain_rows(sums)

        for i, partner in enumerate(partners):
            exchange = pltpu.make_async_remote_copy(
                src_ref=part.at[i], dst_ref=got.at[i], send_sem=send.at[ROUND + i], recv_sem=recv.at[ROUND + i],
                device_id={"dp": partner}, device_id_type=MESH,
            )
            exchange.start()
            exchange.wait()
            if i < rounds - 1:
                part[i + 1] = part[i] + got[i]
            else:
                final[...] = (part[i] + got[i]) * (1.0 / replicas)
        put_gain.start()

    @pl.when(taker)
    def _():
        copy_gain.start()
        copy_fresh_kv.wait_recv()
        load_fkv2 = load(stored_kv.at[0], kv_vm, L_FKV)
        load_fkv2.start()
        load_fkv2.wait()
        prepare(kv_vm, side_vm, 1, 2, keys, values, mask)

        @pl.loop(0, CHUNKS)
        def _(it):
            copy_fresh_q(it).wait_recv()
            bring = load(chunk(stored_q.at[0], it), chunk(own_q, it), L_CHUNK)
            bring.start()
            bring.wait()
            forward_step(it, own_q, side_vm, 1, keys, values, mask, own_cot)
            load(chunk(own_cot, it), chunk(att_out.at[0], it), L_ATT).start()

        load(own_cot, att_out.at[0], L_ATT).wait()
        copy_gkv.wait_send()
        copy_gq.wait_send()
        copy_gain.wait_send()

    @pl.when(giver)
    def _():
        copy_side.wait_send()
        copy_gkv.wait_recv()
        copy_gq.wait_recv()
        copy_gain.wait_recv()

    @pl.when(jnp.logical_not(taker))
    def _():
        copy_cot.wait_send()
        copy_held_kv.wait_send()
        copy_held_q.wait_send()
        copy_att.wait_recv()
        copy_fresh_kv.wait_recv()
        for i in range(CHUNKS):
            copy_fresh_q(i).wait_recv()

    @pl.when(jnp.logical_not(giver))
    def _():
        copy_att.wait_send()
        put_gq.wait()
        put_gkv.wait()
        put_gain.wait()

    copy_fresh_kv.wait_send()
    for i in range(CHUNKS):
        copy_fresh_q(i).wait_send()


def local_tick(sections, replicas, fresh_q, fresh_kv, held_q, held_kv, cot, gains, plan, segment_ids):
    tokens, width, kv_width = fresh_q.shape[1], fresh_q.shape[2], fresh_kv.shape[2]
    ids = [lax.dynamic_slice_in_dim(segment_ids[0], plan[0, i], 1, 0).astype(F32) for i in range(2)]
    ids = jnp.pad(jnp.concatenate(ids, axis=0), ((0, 4), (0, D - tokens)))
    side = jnp.concatenate([gains[0], ids], axis=0)
    rounds = replicas.bit_length() - 1
    wide, narrow = (tokens, width), (tokens, kv_width)
    anywhere = pl.BlockSpec(memory_space=pl.ANY)
    shape = jax.ShapeDtypeStruct
    outs = pl.pallas_call(
        functools.partial(kernel, sections, replicas),
        out_shape=(
            shape((1, *wide), BF16), shape((1, *wide), BF16), shape((1, *narrow), BF16),
            shape((1, *wide), BF16), shape((1, *narrow), BF16), shape((8, D), F32),
        ),
        in_specs=[anywhere] * 6,
        out_specs=(anywhere,) * 6,
        scratch_shapes=[
            pltpu.VMEM(wide, BF16), pltpu.VMEM(narrow, BF16), pltpu.VMEM(wide, BF16),
            pltpu.VMEM(wide, BF16), pltpu.VMEM(narrow, BF16), pltpu.VMEM(wide, BF16),
            pltpu.VMEM(wide, BF16), pltpu.VMEM(narrow, BF16), pltpu.VMEM((2, 8, D), F32),
            pltpu.VMEM(wide, BF16), pltpu.VMEM(narrow, BF16), pltpu.VMEM(wide, BF16),
            pltpu.VMEM(wide, BF16), pltpu.VMEM(narrow, BF16),
            pltpu.VMEM((KV_HEADS, D, D), BF16), pltpu.VMEM((KV_HEADS, D, D), BF16),
            pltpu.VMEM((tokens, D), F32),
            pltpu.VMEM((KV_HEADS, D, D), F32), pltpu.VMEM((KV_HEADS, D, D), F32),
            pltpu.VMEM((2, 8, D), F32),
            pltpu.VMEM((rounds, 2, 8, D), F32), pltpu.VMEM((rounds, 2, 8, D), F32), pltpu.VMEM((2, 8, D), F32),
            pltpu.SemaphoreType.DMA((ROUND + rounds,)),
            pltpu.SemaphoreType.DMA((ROUND + rounds,)),
            pltpu.SemaphoreType.DMA((L_CHUNK + 1,)),
        ],
        compiler_params=pltpu.CompilerParams(collective_id=0, has_side_effects=True, vmem_limit_bytes=VMEM_LIMIT),
    )(fresh_q, fresh_kv, held_q, held_kv, cot, side)
    return (*outs[:5], outs[5][None, :2])


VMEM_LIMIT = 16 * 2**20


def solution(mesh):
    tokens = P("section", "dp", None)
    return jax.shard_map(
        functools.partial(local_tick, mesh.shape["section"], mesh.shape["dp"]),
        mesh=mesh,
        in_specs=(tokens,) * 5 + (P("section", None, None), P("section", None), P("dp", None, None)),
        out_specs=(tokens,) * 5 + (P("section", None, None),),
        check_vma=False,
    )
```

```python
import functools
import math

import jax
import jax.numpy as jnp
from jax import lax
from jax.experimental import pallas as pl
from jax.experimental.pallas import tpu as pltpu
from jax.sharding import PartitionSpec as P

F32, BF16 = jnp.float32, jnp.bfloat16
D = 128
HEADS, KV_HEADS = 16, 2
PER_KV = HEADS // KV_HEADS
PLACES = 4
GROUP = 4
EPSILON = 1e-06
SCALE = 1.0 / math.sqrt(D)
MESH = pl.DeviceIdType.MESH

HELD_KV, HELD_Q, COT, ATT, SIDE, GRAD_Q, GRAD_KV, GAIN, FRESH_KV, FRESH_Q = range(10)
CHUNKS = HEADS // GROUP
ROUND = FRESH_Q + CHUNKS

L_FQ, L_FKV, L_GAINS, L_SEGMENTS, L_PLAN, L_HQ, L_HKV, L_COT, L_GQ, L_GKV, L_GAIN, L_ATT, L_CHUNK = range(13)


def dot(a, b, dims):
    return lax.dot_general(a, b, ((dims[:1], dims[1:]), ((), ())), preferred_element_type=F32)


def lane_sum(a):
    return jnp.sum(a, axis=-1, keepdims=True)


def fold(a):
    return jnp.sum(a.reshape(-1, 8, D), axis=0)


def head(i):
    start = i * D
    return pl.ds(start if isinstance(i, int) else pl.multiple_of(start, D), D)


def prepare(kv, side, slot, row, keys, values, mask):
    tokens = kv.shape[0]
    ids = jnp.broadcast_to(side[slot, row : row + 1, :], (D, D))
    rows = lax.broadcasted_iota(jnp.int32, (D, D), 0)
    cols = lax.broadcasted_iota(jnp.int32, (D, D), 1)
    allowed = jnp.where((ids == ids.T) & (cols <= rows), 1.0, 0.0)
    mask[...] = allowed[:tokens]
    gain = side[slot, 1:2, :]
    pad = jnp.zeros((D - tokens, D), BF16)
    for g in range(KV_HEADS):
        x = kv[:, head(g)].astype(F32)
        r = lax.rsqrt(jnp.mean(x * x, axis=-1, keepdims=True) + EPSILON)
        keys[g, :tokens, :] = (x * r * gain).astype(BF16)
        keys[g, tokens:, :] = pad
        values[g, :tokens, :] = kv[:, head(KV_HEADS + g)]
        values[g, tokens:, :] = pad


def probabilities(q, lanes, gain, k, mask):
    x = q[:, lanes].astype(F32)
    r = lax.rsqrt(jnp.mean(x * x, axis=-1, keepdims=True) + EPSILON)
    qn = (x * r * gain).astype(BF16)
    w = jnp.exp(dot(qn, k, (1, 1)) * SCALE) * mask[...]
    return x, r, qn, w * (1.0 / lane_sum(w))


def forward_step(it, q, side, slot, keys, values, mask, out):
    g = it // (PER_KV // GROUP)
    k, v = keys[g], values[g]
    gain = side[slot, 0:1, :]
    for u in range(GROUP):
        lanes = head(it * GROUP + u)
        p = probabilities(q, lanes, gain, k, mask)[3]
        out[:, lanes] = dot(p.astype(BF16), v, (1, 0)).astype(BF16)


def backward(q, kv, cot, side, slot, keys, values, mask, dk, dv, sums, grad_q, grad_kv):
    tokens = q.shape[0]
    prepare(kv, side, slot, 3, keys, values, mask)
    dk[...] = jnp.zeros_like(dk)
    dv[...] = jnp.zeros_like(dv)
    sums[...] = jnp.zeros_like(sums)

    @pl.loop(0, CHUNKS)
    def _(it):
        g = it // (PER_KV // GROUP)
        k, v = keys[g], values[g]
        gain = side[slot, 0:1, :]
        for u in range(GROUP):
            lanes = head(it * GROUP + u)
            x, r, qn, p = probabilities(q, lanes, gain, k, mask)
            up = cot[:, lanes]
            d_p = dot(up, v, (1, 1))
            dv[g] += dot(p.astype(BF16), up, (0, 0))
            d_s = (p * (d_p - lane_sum(p * d_p))).astype(BF16)
            d_qn = dot(d_s, k, (1, 0)) * SCALE
            dk[g] += dot(d_s, qn, (0, 0))
            scaled = gain * d_qn
            inner = lane_sum(x * scaled) * (1.0 / D)
            grad_q[:, lanes] = (r * scaled - x * (r * r * r * inner)).astype(BF16)
            sums[0] += fold(d_qn * x * r)

    gain = side[slot, 1:2, :]
    for g in range(KV_HEADS):
        x = kv[:, head(g)].astype(F32)
        r = lax.rsqrt(jnp.mean(x * x, axis=-1, keepdims=True) + EPSILON)
        d_kn = dk[g, :tokens, :] * SCALE
        scaled = gain * d_kn
        inner = lane_sum(x * scaled) * (1.0 / D)
        grad_kv[:, head(g)] = (r * scaled - x * (r * r * r * inner)).astype(BF16)
        grad_kv[:, head(KV_HEADS + g)] = dv[g, :tokens, :].astype(BF16)
        sums[1] += fold(d_kn * x * r)


def gain_rows(sums):
    q = jnp.sum(sums[0], axis=0, keepdims=True)
    k = jnp.sum(sums[1], axis=0, keepdims=True)
    row = lax.broadcasted_iota(jnp.int32, (8, D), 0)
    return jnp.where(row == 0, q, jnp.where(row == 1, k, 0.0))


def kernel(
    sections, replicas,
    fresh_q, fresh_kv, held_q, held_kv, cot, gains, plan, segments,
    att_out, stored_q, stored_kv, grad_q_out, grad_kv_out, gain_out,
    q_vm, kv_vm, att_vm, hq_vm, hkv_vm, cot_vm, gq_vm, gkv_vm, side_vm,
    own_q, own_kv, own_cot, far_gq, far_gkv,
    keys, values, mask, dk, dv, sums, part, got, final, gains_vm, segments_vm, plan_sm,
    send, recv, local, gate,
):
    s, d = lax.axis_index("section"), lax.axis_index("dp")
    mirror, up, down = sections - 1 - s, lax.rem(s + 1, sections), lax.rem(s + sections - 1, sections)
    rounds = replicas.bit_length() - 1
    partners = [d + (1 << i) * (1 - 2 * lax.rem(d // (1 << i), 2)) for i in range(rounds)]
    half = sections // 2
    stride = replicas // PLACES
    z = d // stride
    odd = lax.rem(s // (sections // 4), 2)
    place = z + odd * (PLACES - 1 - 2 * z)
    step = stride * (1 - 2 * odd)
    farther = lax.rem(d + step + replicas, replicas)
    nearer = lax.rem(d - step + replicas, replicas)
    giver = (s == half - 1) | (s == sections - 1)
    taker = (s == 0) | (s == half)
    normal = jnp.logical_not(giver | taker)

    def remote(src, dst, slot, section):
        return pltpu.make_async_remote_copy(
            src_ref=src, dst_ref=dst, send_sem=send.at[slot], recv_sem=recv.at[slot],
            device_id={"section": section}, device_id_type=MESH,
        )

    def chunk(ref, i):
        start = i * GROUP * D
        return ref.at[:, pl.ds(start if isinstance(i, int) else pl.multiple_of(start, GROUP * D), GROUP * D)]

    def load(src, dst, slot):
        return pltpu.make_async_copy(src, dst, local.at[slot])

    copy_held_kv = remote(held_kv.at[0], hkv_vm, HELD_KV, mirror)
    copy_held_q = remote(held_q.at[0], hq_vm, HELD_Q, mirror)
    copy_cot = remote(cot.at[0], cot_vm, COT, down)
    copy_att = remote(att_vm, att_out.at[0], ATT, up)
    copy_side = remote(side_vm.at[0], side_vm.at[1], SIDE, mirror)
    copy_gq = remote(far_gq, grad_q_out.at[0], GRAD_Q, mirror)
    copy_gkv = remote(far_gkv, grad_kv_out.at[0], GRAD_KV, mirror)
    copy_gain = remote(final.at[1], gain_out.at[0], GAIN, mirror)
    copy_fresh_kv = remote(fresh_kv.at[0], stored_kv.at[0], FRESH_KV, mirror)

    def copy_fresh_q(i):
        return remote(chunk(fresh_q.at[0], i), chunk(stored_q.at[0], i), FRESH_Q + i, mirror)

    load_fq = load(fresh_q.at[0], q_vm, L_FQ)
    load_fkv = load(fresh_kv.at[0], kv_vm, L_FKV)
    load_gains = load(gains.at[0], gains_vm, L_GAINS)
    load_plan = load(plan, plan_sm, L_PLAN)
    load_segments = load(segments.at[0], segments_vm, L_SEGMENTS)
    load_hq = load(held_q.at[0], own_q, L_HQ)
    load_hkv = load(held_kv.at[0], own_kv, L_HKV)
    load_cot = load(cot.at[0], own_cot, L_COT)
    put_gq = load(gq_vm, grad_q_out.at[0], L_GQ)
    put_gkv = load(gkv_vm, grad_kv_out.at[0], L_GKV)
    put_gain = load(final.at[0], gain_out.at[0], L_GAIN)

    def first_is_out(copies):
        for copy in copies:
            copy.wait_send()

        @pl.when(place > 0)
        def _():
            pl.semaphore_signal(gate, inc=1, device_id={"dp": nearer}, device_id_type=MESH)

    def wait_for_turn():
        @pl.when(place < PLACES - 1)
        def _():
            pl.semaphore_wait(gate, 1)

    fresh_copies = [copy_fresh_kv, *(copy_fresh_q(i) for i in range(CHUNKS))]
    held_copies = [copy_held_kv, copy_held_q]

    barrier = pltpu.get_barrier_semaphore()
    for section in (mirror, up, down):
        pl.semaphore_signal(barrier, inc=1, device_id={"section": section}, device_id_type=MESH)
    for partner in (*partners, farther, nearer):
        pl.semaphore_signal(barrier, inc=1, device_id={"dp": partner}, device_id_type=MESH)

    load_plan.start()
    load_gains.start()
    load_segments.start()

    @pl.when(jnp.logical_not(giver))
    def _():
        load_fkv.start()
        load_fq.start()

    @pl.when(taker)
    def _():
        load_hkv.start()
        load_hq.start()
        load_cot.start()

    load_plan.wait()
    load_gains.wait()
    load_segments.wait()
    side_vm[0] = jnp.zeros((8, D), F32)
    side_vm[0, 0:2, :] = gains_vm[...]
    micro = lax.broadcasted_iota(jnp.int32, segments_vm.shape, 0)
    for i in range(2):
        row = jnp.sum(jnp.where(micro == plan_sm[0, i], segments_vm[...], 0), axis=0, keepdims=True)
        side_vm[0, 2 + i : 3 + i, : segments_vm.shape[1]] = row.astype(F32)

    pl.semaphore_wait(barrier, 5 + rounds)

    @pl.when(giver)
    def _():
        copy_side.start()

    @pl.when(jnp.logical_not(taker))
    def _():
        copy_cot.start()
        copy_held_kv.start()
        copy_held_q.start()

    @pl.when(taker)
    def _():
        for copy in fresh_copies:
            copy.start()

    @pl.when(jnp.logical_not(giver))
    def _():
        load_fkv.wait()
        prepare(kv_vm, side_vm, 0, 2, keys, values, mask)
        load_fq.wait()

        @pl.loop(0, CHUNKS)
        def _(it):
            forward_step(it, q_vm, side_vm, 0, keys, values, mask, att_vm)

        copy_att.start()

    @pl.when(jnp.logical_not(taker))
    def _():
        wait_for_turn()
        for copy in fresh_copies:
            copy.start()
        first_is_out(held_copies)

    @pl.when(taker)
    def _():
        load_hkv.wait()
        load_hq.wait()
        load_cot.wait()
        copy_side.wait_recv()
        backward(own_q, own_kv, own_cot, side_vm, 1, keys, values, mask, dk, dv, sums, far_gq, far_gkv)
        wait_for_turn()
        copy_gkv.start()
        copy_gq.start()
        first_is_out(fresh_copies)
        part[0, 1] = gain_rows(sums)

    @pl.when(normal)
    def _():
        part[0, 1] = jnp.zeros((8, D), F32)

    @pl.when(jnp.logical_not(giver))
    def _():
        copy_cot.wait_recv()
        copy_held_kv.wait_recv()
        copy_held_q.wait_recv()
        backward(hq_vm, hkv_vm, cot_vm, side_vm, 0, keys, values, mask, dk, dv, sums, gq_vm, gkv_vm)
        put_gkv.start()
        put_gq.start()
        part[0, 0] = gain_rows(sums)

        for i, partner in enumerate(partners):
            exchange = pltpu.make_async_remote_copy(
                src_ref=part.at[i], dst_ref=got.at[i], send_sem=send.at[ROUND + i], recv_sem=recv.at[ROUND + i],
                device_id={"dp": partner}, device_id_type=MESH,
            )
            exchange.start()
            exchange.wait()
            if i < rounds - 1:
                part[i + 1] = part[i] + got[i]
            else:
                final[...] = ((part[i] + got[i]) * (1.0 / replicas))[:, :2]
        put_gain.start()

    @pl.when(taker)
    def _():
        copy_gain.start()
        copy_fresh_kv.wait_recv()
        load_fkv2 = load(stored_kv.at[0], kv_vm, L_FKV)
        load_fkv2.start()
        load_fkv2.wait()
        prepare(kv_vm, side_vm, 1, 2, keys, values, mask)

        @pl.loop(0, CHUNKS)
        def _(it):
            copy_fresh_q(it).wait_recv()
            bring = load(chunk(stored_q.at[0], it), chunk(own_q, it), L_CHUNK)
            bring.start()
            bring.wait()
            forward_step(it, own_q, side_vm, 1, keys, values, mask, own_cot)
            load(chunk(own_cot, it), chunk(att_out.at[0], it), L_ATT).start()

        load(own_cot, att_out.at[0], L_ATT).wait()
        copy_gkv.wait_send()
        copy_gq.wait_send()
        copy_gain.wait_send()

    @pl.when(giver)
    def _():
        copy_side.wait_send()
        copy_gkv.wait_recv()
        copy_gq.wait_recv()
        copy_gain.wait_recv()

    @pl.when(jnp.logical_not(taker))
    def _():
        copy_cot.wait_send()
        copy_att.wait_recv()
        for copy in fresh_copies:
            copy.wait_send()
            copy.wait_recv()

    @pl.when(jnp.logical_not(giver))
    def _():
        copy_att.wait_send()
        put_gq.wait()
        put_gkv.wait()
        put_gain.wait()


def in_hbm(x):
    return pltpu.with_memory_space_constraint(x, pltpu.HBM)


def finish(*refs):
    half = len(refs) // 2
    copies = [pltpu.make_async_copy(refs[i], refs[half + i], refs[-1].at[i]) for i in range(half)]
    for copy in copies:
        copy.start()
    for copy in copies:
        copy.wait()


def local_tick(sections, replicas, fresh_q, fresh_kv, held_q, held_kv, cot, gains, plan, segment_ids):
    tokens, width, kv_width = fresh_q.shape[1], fresh_q.shape[2], fresh_kv.shape[2]
    rounds = replicas.bit_length() - 1
    wide, narrow = (tokens, width), (tokens, kv_width)
    anywhere, hbm = pl.BlockSpec(memory_space=pl.ANY), pl.BlockSpec(memory_space=pltpu.HBM)
    shape = jax.ShapeDtypeStruct
    out_shape = (
        shape((1, *wide), BF16), shape((1, *wide), BF16), shape((1, *narrow), BF16),
        shape((1, *wide), BF16), shape((1, *narrow), BF16), shape((1, 2, D), F32),
    )
    outs = pl.pallas_call(
        functools.partial(kernel, sections, replicas),
        out_shape=out_shape,
        in_specs=[hbm] * 8,
        out_specs=(anywhere,) * 6,
        scratch_shapes=[
            pltpu.VMEM(wide, BF16), pltpu.VMEM(narrow, BF16), pltpu.VMEM(wide, BF16),
            pltpu.VMEM(wide, BF16), pltpu.VMEM(narrow, BF16), pltpu.VMEM(wide, BF16),
            pltpu.VMEM(wide, BF16), pltpu.VMEM(narrow, BF16), pltpu.VMEM((2, 8, D), F32),
            pltpu.VMEM(wide, BF16), pltpu.VMEM(narrow, BF16), pltpu.VMEM(wide, BF16),
            pltpu.VMEM(wide, BF16), pltpu.VMEM(narrow, BF16),
            pltpu.VMEM((KV_HEADS, D, D), BF16), pltpu.VMEM((KV_HEADS, D, D), BF16),
            pltpu.VMEM((tokens, D), F32),
            pltpu.VMEM((KV_HEADS, D, D), F32), pltpu.VMEM((KV_HEADS, D, D), F32),
            pltpu.VMEM((2, 8, D), F32),
            pltpu.VMEM((rounds, 2, 8, D), F32), pltpu.VMEM((rounds, 2, 8, D), F32), pltpu.VMEM((2, 2, D), F32),
            pltpu.VMEM((2, D), F32), pltpu.VMEM(segment_ids.shape[1:], jnp.int32), pltpu.SMEM((1, 2), jnp.int32),
            pltpu.SemaphoreType.DMA((ROUND + rounds,)),
            pltpu.SemaphoreType.DMA((ROUND + rounds,)),
            pltpu.SemaphoreType.DMA((L_CHUNK + 1,)),
            pltpu.SemaphoreType.REGULAR,
        ],
        compiler_params=pltpu.CompilerParams(collective_id=0, has_side_effects=True, vmem_limit_bytes=VMEM_LIMIT),
    )(*(in_hbm(x) for x in (fresh_q, fresh_kv, held_q, held_kv, cot, gains, plan, segment_ids)))
    return pl.pallas_call(
        finish,
        out_shape=out_shape,
        in_specs=[anywhere] * 6,
        out_specs=(hbm,) * 6,
        scratch_shapes=[pltpu.SemaphoreType.DMA((6,))],
        compiler_params=pltpu.CompilerParams(vmem_limit_bytes=2**20),
    )(*outs)


VMEM_LIMIT = 16 * 2**20


def solution(mesh):
    tokens = P("section", "dp", None)
    return jax.shard_map(
        functools.partial(local_tick, mesh.shape["section"], mesh.shape["dp"]),
        mesh=mesh,
        in_specs=(tokens,) * 5 + (P("section", None, None), P("section", None), P("dp", None, None)),
        out_specs=(tokens,) * 5 + (P("section", None, None),),
        check_vma=False,
    )
```

```python
import functools
import math

import jax
import jax.numpy as jnp
from jax import lax
from jax.experimental import pallas as pl
from jax.experimental.pallas import tpu as pltpu
from jax.sharding import PartitionSpec as P

F32, BF16 = jnp.float32, jnp.bfloat16
D = 128
HEADS, KV_HEADS = 16, 2
PER_KV = HEADS // KV_HEADS
PLACES = 4
GROUP = 4
EPSILON = 1e-06
SCALE = 1.0 / math.sqrt(D)
MESH = pl.DeviceIdType.MESH

HELD_KV, HELD_Q, COT, ATT, SIDE, GRAD_Q, GRAD_KV, GAIN, FRESH_KV, FRESH_Q = range(10)
CHUNKS = HEADS // GROUP
ROUND = FRESH_Q + CHUNKS

L_FQ, L_FKV, L_GAINS, L_SEGMENTS, L_PLAN, L_HQ, L_HKV, L_COT, L_GQ, L_GKV, L_GAIN, L_ATT, L_CHUNK = range(13)


def dot(a, b, dims):
    return lax.dot_general(a, b, ((dims[:1], dims[1:]), ((), ())), preferred_element_type=F32)


def lane_sum(a):
    return jnp.sum(a, axis=-1, keepdims=True)


def fold(a):
    return jnp.sum(a.reshape(-1, 8, D), axis=0)


def head(i):
    start = i * D
    return pl.ds(start if isinstance(i, int) else pl.multiple_of(start, D), D)


def prepare(kv, side, slot, row, keys, values, mask):
    tokens = kv.shape[0]
    ids = jnp.broadcast_to(side[slot, row : row + 1, :], (D, D))
    rows = lax.broadcasted_iota(jnp.int32, (D, D), 0)
    cols = lax.broadcasted_iota(jnp.int32, (D, D), 1)
    allowed = jnp.where((ids == ids.T) & (cols <= rows), 1.0, 0.0)
    mask[...] = allowed[:tokens]
    gain = side[slot, 1:2, :]
    pad = jnp.zeros((D - tokens, D), BF16)
    for g in range(KV_HEADS):
        x = kv[:, head(g)].astype(F32)
        r = lax.rsqrt(jnp.mean(x * x, axis=-1, keepdims=True) + EPSILON)
        keys[g, :tokens, :] = (x * r * gain).astype(BF16)
        keys[g, tokens:, :] = pad
        values[g, :tokens, :] = kv[:, head(KV_HEADS + g)]
        values[g, tokens:, :] = pad


def probabilities(q, lanes, gain, k, mask):
    x = q[:, lanes].astype(F32)
    r = lax.rsqrt(jnp.mean(x * x, axis=-1, keepdims=True) + EPSILON)
    qn = (x * r * gain).astype(BF16)
    w = jnp.exp(dot(qn, k, (1, 1)) * SCALE) * mask[...]
    return x, r, qn, w * (1.0 / lane_sum(w))


def forward_step(it, q, side, slot, keys, values, mask, out):
    g = it // (PER_KV // GROUP)
    k, v = keys[g], values[g]
    gain = side[slot, 0:1, :]
    for u in range(GROUP):
        lanes = head(it * GROUP + u)
        p = probabilities(q, lanes, gain, k, mask)[3]
        out[:, lanes] = dot(p.astype(BF16), v, (1, 0)).astype(BF16)


def backward(q, kv, cot, side, slot, keys, values, mask, dk, dv, sums, grad_q, grad_kv):
    tokens = q.shape[0]
    prepare(kv, side, slot, 3, keys, values, mask)
    dk[...] = jnp.zeros_like(dk)
    dv[...] = jnp.zeros_like(dv)
    sums[...] = jnp.zeros_like(sums)

    @pl.loop(0, CHUNKS)
    def _(it):
        g = it // (PER_KV // GROUP)
        k, v = keys[g], values[g]
        gain = side[slot, 0:1, :]
        for u in range(GROUP):
            lanes = head(it * GROUP + u)
            x, r, qn, p = probabilities(q, lanes, gain, k, mask)
            up = cot[:, lanes]
            d_p = dot(up, v, (1, 1))
            dv[g] += dot(p.astype(BF16), up, (0, 0))
            d_s = (p * (d_p - lane_sum(p * d_p))).astype(BF16)
            d_qn = dot(d_s, k, (1, 0)) * SCALE
            dk[g] += dot(d_s, qn, (0, 0))
            scaled = gain * d_qn
            inner = lane_sum(x * scaled) * (1.0 / D)
            grad_q[:, lanes] = (r * scaled - x * (r * r * r * inner)).astype(BF16)
            sums[0] += fold(d_qn * x * r)

    gain = side[slot, 1:2, :]
    for g in range(KV_HEADS):
        x = kv[:, head(g)].astype(F32)
        r = lax.rsqrt(jnp.mean(x * x, axis=-1, keepdims=True) + EPSILON)
        d_kn = dk[g, :tokens, :] * SCALE
        scaled = gain * d_kn
        inner = lane_sum(x * scaled) * (1.0 / D)
        grad_kv[:, head(g)] = (r * scaled - x * (r * r * r * inner)).astype(BF16)
        grad_kv[:, head(KV_HEADS + g)] = dv[g, :tokens, :].astype(BF16)
        sums[1] += fold(d_kn * x * r)


def gain_rows(sums):
    return jnp.concatenate([jnp.sum(sums[i], axis=0, keepdims=True) for i in range(2)], axis=0)


def kernel(
    sections, replicas,
    fresh_q, fresh_kv, held_q, held_kv, cot, gains, plan, segments,
    att_out, stored_q, stored_kv, grad_q_out, grad_kv_out, gain_out,
    q_vm, kv_vm, att_vm, hq_vm, hkv_vm, cot_vm, gq_vm, gkv_vm, side_vm,
    own_q, own_kv, own_cot, far_gq, far_gkv,
    keys, values, mask, dk, dv, sums, part, got, final, gains_vm, segments_vm, plan_sm,
    send, recv, local, gate,
):
    s, d = lax.axis_index("section"), lax.axis_index("dp")
    mirror, up, down = sections - 1 - s, lax.rem(s + 1, sections), lax.rem(s + sections - 1, sections)
    rounds = replicas.bit_length() - 1
    partners = [d + (1 << i) * (1 - 2 * lax.rem(d // (1 << i), 2)) for i in range(rounds)]
    half = sections // 2
    stride = replicas // PLACES
    z = d // stride
    even = 1 - lax.rem(s // (sections // 4), 2)
    place = z + even * (PLACES - 1 - 2 * z)
    step = stride * (1 - 2 * even)
    later = lax.rem(d + step + replicas, replicas)
    earlier = lax.rem(d - step + replicas, replicas)
    giver = (s == half - 1) | (s == sections - 1)
    taker = (s == 0) | (s == half)
    normal = jnp.logical_not(giver | taker)

    def remote(src, dst, slot, section):
        return pltpu.make_async_remote_copy(
            src_ref=src, dst_ref=dst, send_sem=send.at[slot], recv_sem=recv.at[slot],
            device_id={"section": section}, device_id_type=MESH,
        )

    def chunk(ref, i):
        start = i * GROUP * D
        return ref.at[:, pl.ds(start if isinstance(i, int) else pl.multiple_of(start, GROUP * D), GROUP * D)]

    def load(src, dst, slot):
        return pltpu.make_async_copy(src, dst, local.at[slot])

    copy_held_kv = remote(held_kv.at[0], hkv_vm, HELD_KV, mirror)
    copy_held_q = remote(held_q.at[0], hq_vm, HELD_Q, mirror)
    copy_cot = remote(cot.at[0], cot_vm, COT, down)
    copy_att = remote(att_vm, att_out.at[0], ATT, up)
    copy_side = remote(side_vm.at[0], side_vm.at[1], SIDE, mirror)
    copy_gq = remote(far_gq, grad_q_out.at[0], GRAD_Q, mirror)
    copy_gkv = remote(far_gkv, grad_kv_out.at[0], GRAD_KV, mirror)
    copy_gain = remote(final.at[1], gain_out.at[0], GAIN, mirror)
    copy_fresh_kv = remote(fresh_kv.at[0], stored_kv.at[0], FRESH_KV, mirror)

    def copy_fresh_q(i):
        return remote(chunk(fresh_q.at[0], i), chunk(stored_q.at[0], i), FRESH_Q + i, mirror)

    load_fq = load(fresh_q.at[0], q_vm, L_FQ)
    load_fkv = load(fresh_kv.at[0], kv_vm, L_FKV)
    load_gains = load(gains.at[0], gains_vm, L_GAINS)
    load_plan = load(plan, plan_sm, L_PLAN)
    load_segments = load(segments.at[0], segments_vm, L_SEGMENTS)
    load_hq = load(held_q.at[0], own_q, L_HQ)
    load_hkv = load(held_kv.at[0], own_kv, L_HKV)
    load_cot = load(cot.at[0], own_cot, L_COT)
    put_gq = load(gq_vm, grad_q_out.at[0], L_GQ)
    put_gkv = load(gkv_vm, grad_kv_out.at[0], L_GKV)
    put_gain = load(final.at[0], gain_out.at[0], L_GAIN)

    def first_is_out(copies):
        for copy in copies:
            copy.wait_send()

        @pl.when(place > 0)
        def _():
            pl.semaphore_signal(gate, inc=1, device_id={"dp": earlier}, device_id_type=MESH)

    def wait_for_turn():
        @pl.when(place < PLACES - 1)
        def _():
            pl.semaphore_wait(gate, 1)

    fresh_copies = [copy_fresh_kv, *(copy_fresh_q(i) for i in range(CHUNKS))]
    held_copies = [copy_held_kv, copy_held_q]

    barrier = pltpu.get_barrier_semaphore()
    for section in (mirror, up, down):
        pl.semaphore_signal(barrier, inc=1, device_id={"section": section}, device_id_type=MESH)
    for partner in (*partners, later, earlier):
        pl.semaphore_signal(barrier, inc=1, device_id={"dp": partner}, device_id_type=MESH)

    load_plan.start()
    load_gains.start()
    load_segments.start()

    @pl.when(jnp.logical_not(giver))
    def _():
        load_fkv.start()
        load_fq.start()

    @pl.when(taker)
    def _():
        load_hkv.start()
        load_hq.start()
        load_cot.start()

    load_plan.wait()
    load_gains.wait()
    load_segments.wait()
    side_vm[0] = jnp.zeros((8, D), F32)
    side_vm[0, 0:2, :] = gains_vm[...]
    micro = lax.broadcasted_iota(jnp.int32, segments_vm.shape, 0)
    for i in range(2):
        row = jnp.sum(jnp.where(micro == plan_sm[0, i], segments_vm[...], 0), axis=0, keepdims=True)
        side_vm[0, 2 + i : 3 + i, : segments_vm.shape[1]] = row.astype(F32)

    pl.semaphore_wait(barrier, 5 + rounds)

    @pl.when(giver)
    def _():
        copy_side.start()

    @pl.when(jnp.logical_not(taker))
    def _():
        copy_cot.start()
        copy_held_kv.start()
        copy_held_q.start()

    @pl.when(taker)
    def _():
        for copy in fresh_copies:
            copy.start()

    @pl.when(jnp.logical_not(giver))
    def _():
        load_fkv.wait()
        prepare(kv_vm, side_vm, 0, 2, keys, values, mask)
        load_fq.wait()

        @pl.loop(0, CHUNKS)
        def _(it):
            forward_step(it, q_vm, side_vm, 0, keys, values, mask, att_vm)

        copy_att.start()

    @pl.when(jnp.logical_not(taker))
    def _():
        wait_for_turn()
        for copy in fresh_copies:
            copy.start()
        first_is_out(held_copies)

    @pl.when(taker)
    def _():
        load_hkv.wait()
        load_hq.wait()
        load_cot.wait()
        copy_side.wait_recv()
        backward(own_q, own_kv, own_cot, side_vm, 1, keys, values, mask, dk, dv, sums, far_gq, far_gkv)
        wait_for_turn()
        copy_gkv.start()
        copy_gq.start()
        first_is_out(fresh_copies)
        part[0, 1] = gain_rows(sums)

    @pl.when(normal)
    def _():
        part[0, 1] = jnp.zeros((2, D), F32)

    @pl.when(jnp.logical_not(giver))
    def _():
        copy_cot.wait_recv()
        copy_held_kv.wait_recv()
        copy_held_q.wait_recv()
        backward(hq_vm, hkv_vm, cot_vm, side_vm, 0, keys, values, mask, dk, dv, sums, gq_vm, gkv_vm)
        put_gkv.start()
        put_gq.start()
        part[0, 0] = gain_rows(sums)

        for i, partner in enumerate(partners):
            exchange = pltpu.make_async_remote_copy(
                src_ref=part.at[i], dst_ref=got.at[i], send_sem=send.at[ROUND + i], recv_sem=recv.at[ROUND + i],
                device_id={"dp": partner}, device_id_type=MESH,
            )
            exchange.start()
            exchange.wait()
            if i < rounds - 1:
                part[i + 1] = part[i] + got[i]
            else:
                final[...] = (part[i] + got[i]) * (1.0 / replicas)
        put_gain.start()

    @pl.when(taker)
    def _():
        copy_gain.start()
        copy_fresh_kv.wait_recv()
        load_fkv2 = load(stored_kv.at[0], kv_vm, L_FKV)
        load_fkv2.start()
        load_fkv2.wait()
        prepare(kv_vm, side_vm, 1, 2, keys, values, mask)

        @pl.loop(0, CHUNKS)
        def _(it):
            copy_fresh_q(it).wait_recv()
            bring = load(chunk(stored_q.at[0], it), chunk(own_q, it), L_CHUNK)
            bring.start()
            bring.wait()
            forward_step(it, own_q, side_vm, 1, keys, values, mask, own_cot)
            load(chunk(own_cot, it), chunk(att_out.at[0], it), L_ATT).start()

        load(own_cot, att_out.at[0], L_ATT).wait()
        copy_gkv.wait_send()
        copy_gq.wait_send()
        copy_gain.wait_send()

    @pl.when(giver)
    def _():
        copy_side.wait_send()
        copy_gkv.wait_recv()
        copy_gq.wait_recv()
        copy_gain.wait_recv()

    @pl.when(jnp.logical_not(taker))
    def _():
        copy_cot.wait_send()
        copy_att.wait_recv()
        for copy in fresh_copies:
            copy.wait_send()
            copy.wait_recv()

    @pl.when(jnp.logical_not(giver))
    def _():
        copy_att.wait_send()
        put_gq.wait()
        put_gkv.wait()
        put_gain.wait()


def in_hbm(x):
    return pltpu.with_memory_space_constraint(x, pltpu.HBM)


def finish(*refs):
    half = len(refs) // 2
    copies = [pltpu.make_async_copy(refs[i], refs[half + i], refs[-1].at[i]) for i in range(half)]
    for copy in copies:
        copy.start()
    for copy in copies:
        copy.wait()


def local_tick(sections, replicas, fresh_q, fresh_kv, held_q, held_kv, cot, gains, plan, segment_ids):
    tokens, width, kv_width = fresh_q.shape[1], fresh_q.shape[2], fresh_kv.shape[2]
    rounds = replicas.bit_length() - 1
    wide, narrow = (tokens, width), (tokens, kv_width)
    anywhere, hbm = pl.BlockSpec(memory_space=pl.ANY), pl.BlockSpec(memory_space=pltpu.HBM)
    shape = jax.ShapeDtypeStruct
    out_shape = (
        shape((1, *wide), BF16), shape((1, *wide), BF16), shape((1, *narrow), BF16),
        shape((1, *wide), BF16), shape((1, *narrow), BF16), shape((1, 2, D), F32),
    )
    outs = pl.pallas_call(
        functools.partial(kernel, sections, replicas),
        out_shape=out_shape,
        in_specs=[hbm] * 8,
        out_specs=(anywhere,) * 6,
        scratch_shapes=[
            pltpu.VMEM(wide, BF16), pltpu.VMEM(narrow, BF16), pltpu.VMEM(wide, BF16),
            pltpu.VMEM(wide, BF16), pltpu.VMEM(narrow, BF16), pltpu.VMEM(wide, BF16),
            pltpu.VMEM(wide, BF16), pltpu.VMEM(narrow, BF16), pltpu.VMEM((2, 8, D), F32),
            pltpu.VMEM(wide, BF16), pltpu.VMEM(narrow, BF16), pltpu.VMEM(wide, BF16),
            pltpu.VMEM(wide, BF16), pltpu.VMEM(narrow, BF16),
            pltpu.VMEM((KV_HEADS, D, D), BF16), pltpu.VMEM((KV_HEADS, D, D), BF16),
            pltpu.VMEM((tokens, D), F32),
            pltpu.VMEM((KV_HEADS, D, D), F32), pltpu.VMEM((KV_HEADS, D, D), F32),
            pltpu.VMEM((2, 8, D), F32),
            pltpu.VMEM((rounds, 2, 2, D), F32), pltpu.VMEM((rounds, 2, 2, D), F32), pltpu.VMEM((2, 2, D), F32),
            pltpu.VMEM((2, D), F32), pltpu.VMEM(segment_ids.shape[1:], jnp.int32), pltpu.SMEM((1, 2), jnp.int32),
            pltpu.SemaphoreType.DMA((ROUND + rounds,)),
            pltpu.SemaphoreType.DMA((ROUND + rounds,)),
            pltpu.SemaphoreType.DMA((L_CHUNK + 1,)),
            pltpu.SemaphoreType.REGULAR,
        ],
        compiler_params=pltpu.CompilerParams(collective_id=0, has_side_effects=True, vmem_limit_bytes=VMEM_LIMIT),
    )(*(in_hbm(x) for x in (fresh_q, fresh_kv, held_q, held_kv, cot, gains, plan, segment_ids)))
    return pl.pallas_call(
        finish,
        out_shape=out_shape,
        in_specs=[anywhere] * 6,
        out_specs=(hbm,) * 6,
        scratch_shapes=[pltpu.SemaphoreType.DMA((6,))],
        compiler_params=pltpu.CompilerParams(vmem_limit_bytes=2**20),
    )(*outs)


VMEM_LIMIT = 16 * 2**20


def solution(mesh):
    tokens = P("section", "dp", None)
    return jax.shard_map(
        functools.partial(local_tick, mesh.shape["section"], mesh.shape["dp"]),
        mesh=mesh,
        in_specs=(tokens,) * 5 + (P("section", None, None), P("section", None), P("dp", None, None)),
        out_specs=(tokens,) * 5 + (P("section", None, None),),
        check_vma=False,
    )
```

```python
import functools
import math

import jax
import jax.numpy as jnp
from jax import lax
from jax.experimental import pallas as pl
from jax.experimental.pallas import tpu as pltpu
from jax.sharding import PartitionSpec as P

F32, BF16 = jnp.float32, jnp.bfloat16
D = 128
HEADS, KV_HEADS = 16, 2
PER_KV = HEADS // KV_HEADS
CORES = 2
PLACES = 4
GROUP = 4
EPSILON = 1e-06
SCALE = 1.0 / math.sqrt(D)
MESH = pl.DeviceIdType.MESH

HELD_KV, HELD_Q, COT, ATT, SIDE, GRAD_Q, GRAD_KV, GAIN, FRESH_KV, FRESH_Q = range(10)
CHUNKS = HEADS // GROUP
ROUND = FRESH_Q + CHUNKS

L_FQ, L_FKV, L_GAINS, L_SEGMENTS, L_PLAN, L_HQ, L_HKV, L_COT, L_GQ, L_GKV, L_GAIN, L_ATT, L_CHUNK = range(13)


def dot(a, b, dims):
    return lax.dot_general(a, b, ((dims[:1], dims[1:]), ((), ())), preferred_element_type=F32)


def lane_sum(a):
    return jnp.sum(a, axis=-1, keepdims=True)


def fold(a):
    return jnp.sum(a.reshape(-1, 8, D), axis=0)


def head(i):
    start = i * D
    return pl.ds(start if isinstance(i, int) else pl.multiple_of(start, D), D)


def prepare(kv, side, slot, row, keys, values, mask):
    tokens = kv.shape[0]
    ids = jnp.broadcast_to(side[slot, row : row + 1, :], (D, D))
    rows = lax.broadcasted_iota(jnp.int32, (D, D), 0)
    cols = lax.broadcasted_iota(jnp.int32, (D, D), 1)
    allowed = jnp.where((ids == ids.T) & (cols <= rows), 1.0, 0.0)
    mask[...] = allowed[:tokens]
    gain = side[slot, 1:2, :]
    pad = jnp.zeros((D - tokens, D), BF16)
    for g in range(KV_HEADS):
        x = kv[:, head(g)].astype(F32)
        r = lax.rsqrt(jnp.mean(x * x, axis=-1, keepdims=True) + EPSILON)
        keys[g, :tokens, :] = (x * r * gain).astype(BF16)
        keys[g, tokens:, :] = pad
        values[g, :tokens, :] = kv[:, head(KV_HEADS + g)]
        values[g, tokens:, :] = pad


def probabilities(q, lanes, gain, k, mask):
    x = q[:, lanes].astype(F32)
    r = lax.rsqrt(jnp.mean(x * x, axis=-1, keepdims=True) + EPSILON)
    qn = (x * r * gain).astype(BF16)
    w = jnp.exp(dot(qn, k, (1, 1)) * SCALE) * mask[...]
    return x, r, qn, w * (1.0 / lane_sum(w))


def forward_step(it, q, side, slot, keys, values, mask, out):
    g = it // (PER_KV // GROUP)
    k, v = keys[g], values[g]
    gain = side[slot, 0:1, :]
    for u in range(GROUP):
        lanes = head(it * GROUP + u)
        p = probabilities(q, lanes, gain, k, mask)[3]
        out[:, lanes] = dot(p.astype(BF16), v, (1, 0)).astype(BF16)


def backward(q, kv, cot, side, slot, keys, values, mask, dk, dv, sums, grad_q, grad_kv):
    tokens = q.shape[0]
    prepare(kv, side, slot, 3, keys, values, mask)
    dk[...] = jnp.zeros_like(dk)
    dv[...] = jnp.zeros_like(dv)
    sums[...] = jnp.zeros_like(sums)

    @pl.loop(0, CHUNKS)
    def _(it):
        g = it // (PER_KV // GROUP)
        k, v = keys[g], values[g]
        gain = side[slot, 0:1, :]
        for u in range(GROUP):
            lanes = head(it * GROUP + u)
            x, r, qn, p = probabilities(q, lanes, gain, k, mask)
            up = cot[:, lanes]
            d_p = dot(up, v, (1, 1))
            dv[g] += dot(p.astype(BF16), up, (0, 0))
            d_s = (p * (d_p - lane_sum(p * d_p))).astype(BF16)
            d_qn = dot(d_s, k, (1, 0)) * SCALE
            dk[g] += dot(d_s, qn, (0, 0))
            scaled = gain * d_qn
            inner = lane_sum(x * scaled) * (1.0 / D)
            grad_q[:, lanes] = (r * scaled - x * (r * r * r * inner)).astype(BF16)
            sums[0] += fold(d_qn * x * r)

    gain = side[slot, 1:2, :]
    for g in range(KV_HEADS):
        x = kv[:, head(g)].astype(F32)
        r = lax.rsqrt(jnp.mean(x * x, axis=-1, keepdims=True) + EPSILON)
        d_kn = dk[g, :tokens, :] * SCALE
        scaled = gain * d_kn
        inner = lane_sum(x * scaled) * (1.0 / D)
        grad_kv[:, head(g)] = (r * scaled - x * (r * r * r * inner)).astype(BF16)
        grad_kv[:, head(KV_HEADS + g)] = dv[g, :tokens, :].astype(BF16)
        sums[1] += fold(d_kn * x * r)


def gain_rows(sums):
    return jnp.concatenate([jnp.sum(sums[i], axis=0, keepdims=True) for i in range(2)], axis=0)


def kernel(
    sections, replicas,
    fresh_q, fresh_kv, held_q, held_kv, cot, gains, plan, segments,
    att_out, stored_q, stored_kv, grad_q_out, grad_kv_out, gain_out,
    q_vm, kv_vm, att_vm, hq_vm, hkv_vm, cot_vm, gq_vm, gkv_vm, side_vm,
    own_q, own_kv, own_cot, far_gq, far_gkv,
    keys, values, mask, dk, dv, sums, part, around, final, gains_vm, segments_vm, plan_sm,
    send, recv, local, gate,
):
    s, d = lax.axis_index("section"), lax.axis_index("dp")
    mirror, up, down = sections - 1 - s, lax.rem(s + 1, sections), lax.rem(s + sections - 1, sections)
    half = sections // 2
    stride = replicas // PLACES
    z = d // stride
    even = 1 - lax.rem(s // (sections // 4), 2)
    ring = replicas // PLACES // CORES
    core, y = lax.rem(d, CORES), lax.rem(d // CORES, ring)
    other = d + 1 - 2 * core
    right = d + CORES * (lax.rem(y + 1, ring) - y)
    left = d + CORES * (lax.rem(y + ring - 1, ring) - y)
    pair = d + stride * (1 - 2 * lax.rem(z, 2))
    middle = (z > 0) & (z < PLACES - 1)
    place = z + even * (PLACES - 1 - 2 * z)
    step = stride * (1 - 2 * even)
    later = lax.rem(d + step + replicas, replicas)
    earlier = lax.rem(d - step + replicas, replicas)
    giver = (s == half - 1) | (s == sections - 1)
    taker = (s == 0) | (s == half)
    normal = jnp.logical_not(giver | taker)

    def remote(src, dst, slot, section):
        return pltpu.make_async_remote_copy(
            src_ref=src, dst_ref=dst, send_sem=send.at[slot], recv_sem=recv.at[slot],
            device_id={"section": section}, device_id_type=MESH,
        )

    def chunk(ref, i):
        start = i * GROUP * D
        return ref.at[:, pl.ds(start if isinstance(i, int) else pl.multiple_of(start, GROUP * D), GROUP * D)]

    def load(src, dst, slot):
        return pltpu.make_async_copy(src, dst, local.at[slot])

    copy_held_kv = remote(held_kv.at[0], hkv_vm, HELD_KV, mirror)
    copy_held_q = remote(held_q.at[0], hq_vm, HELD_Q, mirror)
    copy_cot = remote(cot.at[0], cot_vm, COT, down)
    copy_att = remote(att_vm, att_out.at[0], ATT, up)
    copy_side = remote(side_vm.at[0], side_vm.at[1], SIDE, mirror)
    copy_gq = remote(far_gq, grad_q_out.at[0], GRAD_Q, mirror)
    copy_gkv = remote(far_gkv, grad_kv_out.at[0], GRAD_KV, mirror)
    copy_gain = remote(final.at[1], gain_out.at[0], GAIN, mirror)
    copy_fresh_kv = remote(fresh_kv.at[0], stored_kv.at[0], FRESH_KV, mirror)

    def copy_fresh_q(i):
        return remote(chunk(fresh_q.at[0], i), chunk(stored_q.at[0], i), FRESH_Q + i, mirror)

    load_fq = load(fresh_q.at[0], q_vm, L_FQ)
    load_fkv = load(fresh_kv.at[0], kv_vm, L_FKV)
    load_gains = load(gains.at[0], gains_vm, L_GAINS)
    load_plan = load(plan, plan_sm, L_PLAN)
    load_segments = load(segments.at[0], segments_vm, L_SEGMENTS)
    load_hq = load(held_q.at[0], own_q, L_HQ)
    load_hkv = load(held_kv.at[0], own_kv, L_HKV)
    load_cot = load(cot.at[0], own_cot, L_COT)
    put_gq = load(gq_vm, grad_q_out.at[0], L_GQ)
    put_gkv = load(gkv_vm, grad_kv_out.at[0], L_GKV)
    put_gain = load(final.at[0], gain_out.at[0], L_GAIN)

    def free_the_earlier():
        @pl.when(place > 0)
        def _():
            pl.semaphore_signal(gate, inc=1, device_id={"dp": earlier}, device_id_type=MESH)

    def wait_for_turn():
        @pl.when(place < PLACES - 1)
        def _():
            pl.semaphore_wait(gate, 1)

    fresh_copies = [copy_fresh_kv, *(copy_fresh_q(i) for i in range(CHUNKS))]
    held_copies = [copy_held_kv, copy_held_q]

    barrier = pltpu.get_barrier_semaphore()
    for section in (mirror, up, down):
        pl.semaphore_signal(barrier, inc=1, device_id={"section": section}, device_id_type=MESH)
    for partner in (other, right, left):
        pl.semaphore_signal(barrier, inc=1, device_id={"dp": partner}, device_id_type=MESH)

    @pl.when(z > 0)
    def _():
        pl.semaphore_signal(barrier, inc=1, device_id={"dp": d - stride}, device_id_type=MESH)

    @pl.when(z < PLACES - 1)
    def _():
        pl.semaphore_signal(barrier, inc=1, device_id={"dp": d + stride}, device_id_type=MESH)

    load_plan.start()
    load_gains.start()
    load_segments.start()

    @pl.when(jnp.logical_not(giver))
    def _():
        load_fkv.start()
        load_fq.start()

    @pl.when(taker)
    def _():
        load_hkv.start()
        load_hq.start()
        load_cot.start()

    load_plan.wait()
    load_gains.wait()
    load_segments.wait()
    side_vm[0] = jnp.zeros((8, D), F32)
    side_vm[0, 0:2, :] = gains_vm[...]
    micro = lax.broadcasted_iota(jnp.int32, segments_vm.shape, 0)
    for i in range(2):
        row = jnp.sum(jnp.where(micro == plan_sm[0, i], segments_vm[...], 0), axis=0, keepdims=True)
        side_vm[0, 2 + i : 3 + i, : segments_vm.shape[1]] = row.astype(F32)

    pl.semaphore_wait(barrier, 6 + jnp.where(z > 0, 1, 0) + jnp.where(z < PLACES - 1, 1, 0))

    @pl.when(giver)
    def _():
        copy_side.start()

    waiting = (s == sections - sections // 4) & (place < PLACES // 2)

    @pl.when(jnp.logical_not(taker))
    def _():
        for copy in held_copies:
            copy.start()

    @pl.when(jnp.logical_not(taker | waiting))
    def _():
        copy_cot.start()

    @pl.when(taker)
    def _():
        for copy in fresh_copies:
            copy.start()

    @pl.when(jnp.logical_not(giver))
    def _():
        load_fkv.wait()
        prepare(kv_vm, side_vm, 0, 2, keys, values, mask)
        load_fq.wait()

        @pl.loop(0, CHUNKS)
        def _(it):
            forward_step(it, q_vm, side_vm, 0, keys, values, mask, att_vm)

        copy_att.start()

    @pl.when(jnp.logical_not(taker))
    def _():
        @pl.when(waiting)
        def _():
            for copy in held_copies:
                copy.wait_send()
            copy_cot.start()

        wait_for_turn()
        for copy in fresh_copies:
            copy.start()

        @pl.when(jnp.logical_not(waiting))
        def _():
            for copy in held_copies:
                copy.wait_send()

        free_the_earlier()

    @pl.when(taker)
    def _():
        load_hkv.wait()
        load_hq.wait()
        load_cot.wait()
        copy_side.wait_recv()
        backward(own_q, own_kv, own_cot, side_vm, 1, keys, values, mask, dk, dv, sums, far_gq, far_gkv)
        wait_for_turn()
        copy_gkv.start()
        copy_gq.start()
        for copy in fresh_copies:
            copy.wait_send()
        free_the_earlier()
        part[0, 1] = gain_rows(sums)

    @pl.when(normal)
    def _():
        part[0, 1] = jnp.zeros((2, D), F32)

    @pl.when(jnp.logical_not(giver))
    def _():
        copy_cot.wait_recv()
        copy_held_kv.wait_recv()
        copy_held_q.wait_recv()
        backward(hq_vm, hkv_vm, cot_vm, side_vm, 0, keys, values, mask, dk, dv, sums, gq_vm, gkv_vm)
        put_gkv.start()
        put_gq.start()
        part[0, 0] = gain_rows(sums)

        def along_dp(src, dst, slot, device):
            return pltpu.make_async_remote_copy(
                src_ref=src, dst_ref=dst, send_sem=send.at[ROUND + slot], recv_sem=recv.at[ROUND + slot],
                device_id={"dp": device}, device_id_type=MESH,
            )

        cores = along_dp(part.at[0], part.at[1], 0, other)
        cores.start()
        cores.wait()
        around[y] = part[0] + part[1]
        sent = []
        for k in range(ring // 2):
            block = around.at[lax.rem(y + ring - k, ring)]
            steps = [along_dp(block, block, 1 + k, right)]
            if k < ring // 2 - 1:
                block = around.at[lax.rem(y + k, ring)]
                steps.append(along_dp(block, block, 1 + ring // 2 + k, left))
            for step_copy in steps:
                step_copy.start()
            for step_copy in steps:
                step_copy.wait_recv()
            sent += steps
        total = around[0]
        for k in range(1, ring):
            total += around[k]
        if PLACES == 1:
            final[...] = total * (1.0 / replicas)
        else:
            part[2] = total
            first = along_dp(part.at[2], part.at[3], ring, pair)
            first.start()
            first.wait_recv()
            second = along_dp(part.at[4], part.at[5], ring + 1, jnp.where(z == 1, d + stride, d - stride))
            third = along_dp(part.at[6], part.at[7], ring + 2, pair)

            @pl.when(middle)
            def _():
                part[4] = part[2] + part[3]
                second.start()
                second.wait_recv()
                part[6] = part[4] + part[5]
                third.start()
                final[...] = part[6] * (1.0 / replicas)
                second.wait_send()
                third.wait_send()

            @pl.when(jnp.logical_not(middle))
            def _():
                third.wait_recv()
                final[...] = part[7] * (1.0 / replicas)

            sent.append(first)
        for step_copy in sent:
            step_copy.wait_send()
        put_gain.start()

    @pl.when(taker)
    def _():
        copy_gain.start()
        copy_fresh_kv.wait_recv()
        load_fkv2 = load(stored_kv.at[0], kv_vm, L_FKV)
        load_fkv2.start()
        load_fkv2.wait()
        prepare(kv_vm, side_vm, 1, 2, keys, values, mask)

        @pl.loop(0, CHUNKS)
        def _(it):
            copy_fresh_q(it).wait_recv()
            bring = load(chunk(stored_q.at[0], it), chunk(own_q, it), L_CHUNK)
            bring.start()
            bring.wait()
            forward_step(it, own_q, side_vm, 1, keys, values, mask, own_cot)
            load(chunk(own_cot, it), chunk(att_out.at[0], it), L_ATT).start()

        load(own_cot, att_out.at[0], L_ATT).wait()
        copy_gkv.wait_send()
        copy_gq.wait_send()
        copy_gain.wait_send()

    @pl.when(giver)
    def _():
        copy_side.wait_send()
        copy_gkv.wait_recv()
        copy_gq.wait_recv()
        copy_gain.wait_recv()

    @pl.when(jnp.logical_not(taker))
    def _():
        copy_cot.wait_send()
        copy_att.wait_recv()
        for copy in fresh_copies:
            copy.wait_send()
            copy.wait_recv()

    @pl.when(jnp.logical_not(giver))
    def _():
        copy_att.wait_send()
        put_gq.wait()
        put_gkv.wait()
        put_gain.wait()


def in_hbm(x):
    return pltpu.with_memory_space_constraint(x, pltpu.HBM)


def finish(*refs):
    half = len(refs) // 2
    copies = [pltpu.make_async_copy(refs[i], refs[half + i], refs[-1].at[i]) for i in range(half)]
    for copy in copies:
        copy.start()
    for copy in copies:
        copy.wait()


def local_tick(sections, replicas, fresh_q, fresh_kv, held_q, held_kv, cot, gains, plan, segment_ids):
    tokens, width, kv_width = fresh_q.shape[1], fresh_q.shape[2], fresh_kv.shape[2]
    ring = replicas // PLACES // CORES
    wide, narrow = (tokens, width), (tokens, kv_width)
    anywhere, hbm = pl.BlockSpec(memory_space=pl.ANY), pl.BlockSpec(memory_space=pltpu.HBM)
    shape = jax.ShapeDtypeStruct
    out_shape = (
        shape((1, *wide), BF16), shape((1, *wide), BF16), shape((1, *narrow), BF16),
        shape((1, *wide), BF16), shape((1, *narrow), BF16), shape((1, 2, D), F32),
    )
    outs = pl.pallas_call(
        functools.partial(kernel, sections, replicas),
        out_shape=out_shape,
        in_specs=[hbm] * 8,
        out_specs=(anywhere,) * 6,
        scratch_shapes=[
            pltpu.VMEM(wide, BF16), pltpu.VMEM(narrow, BF16), pltpu.VMEM(wide, BF16),
            pltpu.VMEM(wide, BF16), pltpu.VMEM(narrow, BF16), pltpu.VMEM(wide, BF16),
            pltpu.VMEM(wide, BF16), pltpu.VMEM(narrow, BF16), pltpu.VMEM((2, 8, D), F32),
            pltpu.VMEM(wide, BF16), pltpu.VMEM(narrow, BF16), pltpu.VMEM(wide, BF16),
            pltpu.VMEM(wide, BF16), pltpu.VMEM(narrow, BF16),
            pltpu.VMEM((KV_HEADS, D, D), BF16), pltpu.VMEM((KV_HEADS, D, D), BF16),
            pltpu.VMEM((tokens, D), F32),
            pltpu.VMEM((KV_HEADS, D, D), F32), pltpu.VMEM((KV_HEADS, D, D), F32),
            pltpu.VMEM((2, 8, D), F32),
            pltpu.VMEM((8, 2, 2, D), F32), pltpu.VMEM((ring, 2, 2, D), F32), pltpu.VMEM((2, 2, D), F32),
            pltpu.VMEM((2, D), F32), pltpu.VMEM(segment_ids.shape[1:], jnp.int32), pltpu.SMEM((1, 2), jnp.int32),
            pltpu.SemaphoreType.DMA((ROUND + ring + 3,)),
            pltpu.SemaphoreType.DMA((ROUND + ring + 3,)),
            pltpu.SemaphoreType.DMA((L_CHUNK + 1,)),
            pltpu.SemaphoreType.REGULAR,
        ],
        compiler_params=pltpu.CompilerParams(collective_id=0, has_side_effects=True, vmem_limit_bytes=VMEM_LIMIT),
    )(*(in_hbm(x) for x in (fresh_q, fresh_kv, held_q, held_kv, cot, gains, plan, segment_ids)))
    return pl.pallas_call(
        finish,
        out_shape=out_shape,
        in_specs=[anywhere] * 6,
        out_specs=(hbm,) * 6,
        scratch_shapes=[pltpu.SemaphoreType.DMA((6,))],
        compiler_params=pltpu.CompilerParams(vmem_limit_bytes=2**20),
    )(*outs)


VMEM_LIMIT = 16 * 2**20


def solution(mesh):
    tokens = P("section", "dp", None)
    return jax.shard_map(
        functools.partial(local_tick, mesh.shape["section"], mesh.shape["dp"]),
        mesh=mesh,
        in_specs=(tokens,) * 5 + (P("section", None, None), P("section", None), P("dp", None, None)),
        out_specs=(tokens,) * 5 + (P("section", None, None),),
        check_vma=False,
    )
```

```python
import functools
import math

import jax
import jax.numpy as jnp
from jax import lax
from jax.experimental import pallas as pl
from jax.experimental.pallas import tpu as pltpu
from jax.sharding import PartitionSpec as P

F32, BF16 = jnp.float32, jnp.bfloat16
D = 128
HEADS, KV_HEADS = 16, 2
PER_KV = HEADS // KV_HEADS
CORES = 2
PLACES = 4
GROUP = 4
EPSILON = 1e-06
SCALE = 1.0 / math.sqrt(D)
MESH = pl.DeviceIdType.MESH

HELD_KV, HELD_Q, COT, ATT, SIDE, GRAD_Q, GRAD_KV, GAIN, FRESH_KV, FRESH_Q = range(10)
CHUNKS = HEADS // GROUP
ROUND = FRESH_Q + CHUNKS

L_FQ, L_FKV, L_GAINS, L_SEGMENTS, L_PLAN, L_HQ, L_HKV, L_COT, L_GQ, L_GKV, L_GAIN, L_ATT, L_CHUNK = range(13)


def dot(a, b, dims):
    return lax.dot_general(a, b, ((dims[:1], dims[1:]), ((), ())), preferred_element_type=F32)


def lane_sum(a):
    return jnp.sum(a, axis=-1, keepdims=True)


def fold(a):
    return jnp.sum(a.reshape(-1, 8, D), axis=0)


def head(i):
    start = i * D
    return pl.ds(start if isinstance(i, int) else pl.multiple_of(start, D), D)


def prepare(kv, side, slot, row, keys, values, mask):
    tokens = kv.shape[0]
    ids = jnp.broadcast_to(side[slot, row : row + 1, :], (D, D))
    rows = lax.broadcasted_iota(jnp.int32, (D, D), 0)
    cols = lax.broadcasted_iota(jnp.int32, (D, D), 1)
    allowed = jnp.where((ids == ids.T) & (cols <= rows), 1.0, 0.0)
    mask[...] = allowed[:tokens]
    gain = side[slot, 1:2, :]
    pad = jnp.zeros((D - tokens, D), BF16)
    for g in range(KV_HEADS):
        x = kv[:, head(g)].astype(F32)
        r = lax.rsqrt(jnp.mean(x * x, axis=-1, keepdims=True) + EPSILON)
        keys[g, :tokens, :] = (x * r * gain).astype(BF16)
        keys[g, tokens:, :] = pad
        values[g, :tokens, :] = kv[:, head(KV_HEADS + g)]
        values[g, tokens:, :] = pad


def probabilities(q, lanes, gain, k, mask):
    x = q[:, lanes].astype(F32)
    r = lax.rsqrt(jnp.mean(x * x, axis=-1, keepdims=True) + EPSILON)
    qn = (x * r * gain).astype(BF16)
    w = jnp.exp(dot(qn, k, (1, 1)) * SCALE) * mask[...]
    return x, r, qn, w * (1.0 / lane_sum(w))


def forward_step(it, q, side, slot, keys, values, mask, out):
    g = it // (PER_KV // GROUP)
    k, v = keys[g], values[g]
    gain = side[slot, 0:1, :]
    for u in range(GROUP):
        lanes = head(it * GROUP + u)
        p = probabilities(q, lanes, gain, k, mask)[3]
        out[:, lanes] = dot(p.astype(BF16), v, (1, 0)).astype(BF16)


def backward(q, kv, cot, side, slot, keys, values, mask, dk, dv, sums, grad_q, grad_kv):
    tokens = q.shape[0]
    prepare(kv, side, slot, 3, keys, values, mask)
    dk[...] = jnp.zeros_like(dk)
    dv[...] = jnp.zeros_like(dv)
    sums[...] = jnp.zeros_like(sums)

    @pl.loop(0, CHUNKS)
    def _(it):
        g = it // (PER_KV // GROUP)
        k, v = keys[g], values[g]
        gain = side[slot, 0:1, :]
        for u in range(GROUP):
            lanes = head(it * GROUP + u)
            x, r, qn, p = probabilities(q, lanes, gain, k, mask)
            up = cot[:, lanes]
            d_p = dot(up, v, (1, 1))
            dv[g] += dot(p.astype(BF16), up, (0, 0))
            d_s = (p * (d_p - lane_sum(p * d_p))).astype(BF16)
            d_qn = dot(d_s, k, (1, 0)) * SCALE
            dk[g] += dot(d_s, qn, (0, 0))
            scaled = gain * d_qn
            inner = lane_sum(x * scaled) * (1.0 / D)
            grad_q[:, lanes] = (r * scaled - x * (r * r * r * inner)).astype(BF16)
            sums[0] += fold(d_qn * x * r)

    gain = side[slot, 1:2, :]
    for g in range(KV_HEADS):
        x = kv[:, head(g)].astype(F32)
        r = lax.rsqrt(jnp.mean(x * x, axis=-1, keepdims=True) + EPSILON)
        d_kn = dk[g, :tokens, :] * SCALE
        scaled = gain * d_kn
        inner = lane_sum(x * scaled) * (1.0 / D)
        grad_kv[:, head(g)] = (r * scaled - x * (r * r * r * inner)).astype(BF16)
        grad_kv[:, head(KV_HEADS + g)] = dv[g, :tokens, :].astype(BF16)
        sums[1] += fold(d_kn * x * r)


def gain_rows(sums):
    return jnp.concatenate([jnp.sum(sums[i], axis=0, keepdims=True) for i in range(2)], axis=0)


def kernel(
    sections, replicas,
    fresh_q, fresh_kv, held_q, held_kv, cot, gains, plan, segments,
    att_out, stored_q, stored_kv, grad_q_out, grad_kv_out, gain_out,
    q_vm, kv_vm, att_vm, hq_vm, hkv_vm, cot_vm, gq_vm, gkv_vm, side_vm,
    own_q, own_kv, own_cot, far_gq, far_gkv,
    keys, values, mask, dk, dv, sums, part, around, final, gains_vm, segments_vm, plan_sm,
    send, recv, local, gate,
):
    s, d = lax.axis_index("section"), lax.axis_index("dp")
    mirror, up, down = sections - 1 - s, lax.rem(s + 1, sections), lax.rem(s + sections - 1, sections)
    half = sections // 2
    stride = replicas // PLACES
    z = d // stride
    even = 1 - lax.rem(s // (sections // 4), 2)
    ring = replicas // PLACES // CORES
    core, y = lax.rem(d, CORES), lax.rem(d // CORES, ring)
    other = d + 1 - 2 * core
    right = d + CORES * (lax.rem(y + 1, ring) - y)
    left = d + CORES * (lax.rem(y + ring - 1, ring) - y)
    pair = d + stride * (1 - 2 * lax.rem(z, 2))
    middle = (z > 0) & (z < PLACES - 1)
    place = z + even * (PLACES - 1 - 2 * z)
    step = stride * (1 - 2 * even)
    later = lax.rem(d + step + replicas, replicas)
    earlier = lax.rem(d - step + replicas, replicas)
    giver = (s == half - 1) | (s == sections - 1)
    taker = (s == 0) | (s == half)
    normal = jnp.logical_not(giver | taker)

    def remote(src, dst, slot, section):
        return pltpu.make_async_remote_copy(
            src_ref=src, dst_ref=dst, send_sem=send.at[slot], recv_sem=recv.at[slot],
            device_id={"section": section}, device_id_type=MESH,
        )

    def chunk(ref, i):
        start = i * GROUP * D
        return ref.at[:, pl.ds(start if isinstance(i, int) else pl.multiple_of(start, GROUP * D), GROUP * D)]

    def load(src, dst, slot):
        return pltpu.make_async_copy(src, dst, local.at[slot])

    copy_held_kv = remote(held_kv.at[0], hkv_vm, HELD_KV, mirror)
    copy_held_q = remote(held_q.at[0], hq_vm, HELD_Q, mirror)
    copy_cot = remote(cot.at[0], cot_vm, COT, down)
    copy_att = remote(att_vm, att_out.at[0], ATT, up)
    copy_side = remote(side_vm.at[0], side_vm.at[1], SIDE, mirror)
    copy_gq = remote(far_gq, grad_q_out.at[0], GRAD_Q, mirror)
    copy_gkv = remote(far_gkv, grad_kv_out.at[0], GRAD_KV, mirror)
    copy_gain = remote(final.at[1], gain_out.at[0], GAIN, mirror)
    copy_fresh_kv = remote(fresh_kv.at[0], stored_kv.at[0], FRESH_KV, mirror)

    def copy_fresh_q(i):
        return remote(chunk(fresh_q.at[0], i), chunk(stored_q.at[0], i), FRESH_Q + i, mirror)

    load_fq = load(fresh_q.at[0], q_vm, L_FQ)
    load_fkv = load(fresh_kv.at[0], kv_vm, L_FKV)
    load_gains = load(gains.at[0], gains_vm, L_GAINS)
    load_plan = load(plan, plan_sm, L_PLAN)
    load_segments = load(segments.at[0], segments_vm, L_SEGMENTS)
    load_hq = load(held_q.at[0], own_q, L_HQ)
    load_hkv = load(held_kv.at[0], own_kv, L_HKV)
    load_cot = load(cot.at[0], own_cot, L_COT)
    put_gq = load(gq_vm, grad_q_out.at[0], L_GQ)
    put_gkv = load(gkv_vm, grad_kv_out.at[0], L_GKV)
    put_gain = load(final.at[0], gain_out.at[0], L_GAIN)

    def free_the_earlier():
        @pl.when(place > 0)
        def _():
            pl.semaphore_signal(gate, inc=1, device_id={"dp": earlier}, device_id_type=MESH)

    def wait_for_turn():
        @pl.when(place < PLACES - 1)
        def _():
            pl.semaphore_wait(gate, 1)

    fresh_copies = [copy_fresh_kv, *(copy_fresh_q(i) for i in range(CHUNKS))]
    held_copies = [copy_held_kv, copy_held_q]

    barrier = pltpu.get_barrier_semaphore()
    for section in (mirror, up, down):
        pl.semaphore_signal(barrier, inc=1, device_id={"section": section}, device_id_type=MESH)
    for partner in (other, right, left):
        pl.semaphore_signal(barrier, inc=1, device_id={"dp": partner}, device_id_type=MESH)

    @pl.when(z > 0)
    def _():
        pl.semaphore_signal(barrier, inc=1, device_id={"dp": d - stride}, device_id_type=MESH)

    @pl.when(z < PLACES - 1)
    def _():
        pl.semaphore_signal(barrier, inc=1, device_id={"dp": d + stride}, device_id_type=MESH)

    load_plan.start()
    load_gains.start()
    load_segments.start()

    @pl.when(jnp.logical_not(giver))
    def _():
        load_fkv.start()
        load_fq.start()

    @pl.when(taker)
    def _():
        load_hkv.start()
        load_hq.start()
        load_cot.start()

    load_plan.wait()
    load_gains.wait()
    load_segments.wait()
    side_vm[0] = jnp.zeros((8, D), F32)
    side_vm[0, 0:2, :] = gains_vm[...]
    micro = lax.broadcasted_iota(jnp.int32, segments_vm.shape, 0)
    for i in range(2):
        row = jnp.sum(jnp.where(micro == plan_sm[0, i], segments_vm[...], 0), axis=0, keepdims=True)
        side_vm[0, 2 + i : 3 + i, : segments_vm.shape[1]] = row.astype(F32)

    pl.semaphore_wait(barrier, 6 + jnp.where(z > 0, 1, 0) + jnp.where(z < PLACES - 1, 1, 0))

    @pl.when(giver)
    def _():
        copy_side.start()

    waiting = (lax.rem(s, sections // 4) == 0) & (place < jnp.where(s == sections - sections // 4, PLACES // 2, 1))

    @pl.when(jnp.logical_not(taker))
    def _():
        for copy in held_copies:
            copy.start()

    @pl.when(jnp.logical_not(taker | waiting))
    def _():
        copy_cot.start()

    @pl.when(taker)
    def _():
        for copy in fresh_copies:
            copy.start()

    @pl.when(jnp.logical_not(giver))
    def _():
        load_fkv.wait()
        prepare(kv_vm, side_vm, 0, 2, keys, values, mask)
        load_fq.wait()

        @pl.loop(0, CHUNKS)
        def _(it):
            forward_step(it, q_vm, side_vm, 0, keys, values, mask, att_vm)

        copy_att.start()

    @pl.when(jnp.logical_not(taker))
    def _():
        @pl.when(waiting)
        def _():
            for copy in held_copies:
                copy.wait_send()
            copy_cot.start()

        wait_for_turn()
        for copy in fresh_copies:
            copy.start()

        @pl.when(jnp.logical_not(waiting))
        def _():
            for copy in held_copies:
                copy.wait_send()

        free_the_earlier()

    @pl.when(taker)
    def _():
        load_hkv.wait()
        load_hq.wait()
        load_cot.wait()
        copy_side.wait_recv()
        backward(own_q, own_kv, own_cot, side_vm, 1, keys, values, mask, dk, dv, sums, far_gq, far_gkv)
        wait_for_turn()
        copy_gkv.start()
        copy_gq.start()
        for copy in fresh_copies:
            copy.wait_send()
        free_the_earlier()
        part[0, 1] = gain_rows(sums)

    @pl.when(normal)
    def _():
        part[0, 1] = jnp.zeros((2, D), F32)

    @pl.when(jnp.logical_not(giver))
    def _():
        copy_cot.wait_recv()
        copy_held_kv.wait_recv()
        copy_held_q.wait_recv()
        backward(hq_vm, hkv_vm, cot_vm, side_vm, 0, keys, values, mask, dk, dv, sums, gq_vm, gkv_vm)
        put_gkv.start()
        put_gq.start()
        part[0, 0] = gain_rows(sums)

        def along_dp(src, dst, slot, device):
            return pltpu.make_async_remote_copy(
                src_ref=src, dst_ref=dst, send_sem=send.at[ROUND + slot], recv_sem=recv.at[ROUND + slot],
                device_id={"dp": device}, device_id_type=MESH,
            )

        cores = along_dp(part.at[0], part.at[1], 0, other)
        cores.start()
        cores.wait()
        around[y] = part[0] + part[1]
        sent = []
        for k in range(ring // 2):
            block = around.at[lax.rem(y + ring - k, ring)]
            steps = [along_dp(block, block, 1 + k, right)]
            if k < ring // 2 - 1:
                block = around.at[lax.rem(y + k, ring)]
                steps.append(along_dp(block, block, 1 + ring // 2 + k, left))
            for step_copy in steps:
                step_copy.start()
            for step_copy in steps:
                step_copy.wait_recv()
            sent += steps
        total = around[0]
        for k in range(1, ring):
            total += around[k]
        if PLACES == 1:
            final[...] = total * (1.0 / replicas)
        else:
            part[2] = total
            first = along_dp(part.at[2], part.at[3], ring, pair)
            first.start()
            first.wait_recv()
            second = along_dp(part.at[4], part.at[5], ring + 1, jnp.where(z == 1, d + stride, d - stride))
            third = along_dp(part.at[6], part.at[7], ring + 2, pair)

            @pl.when(middle)
            def _():
                part[4] = part[2] + part[3]
                second.start()
                second.wait_recv()
                part[6] = part[4] + part[5]
                third.start()
                final[...] = part[6] * (1.0 / replicas)
                second.wait_send()
                third.wait_send()

            @pl.when(jnp.logical_not(middle))
            def _():
                third.wait_recv()
                final[...] = part[7] * (1.0 / replicas)

            sent.append(first)
        for step_copy in sent:
            step_copy.wait_send()
        put_gain.start()

    @pl.when(taker)
    def _():
        copy_gain.start()
        copy_fresh_kv.wait_recv()
        load_fkv2 = load(stored_kv.at[0], kv_vm, L_FKV)
        load_fkv2.start()
        load_fkv2.wait()
        prepare(kv_vm, side_vm, 1, 2, keys, values, mask)

        @pl.loop(0, CHUNKS)
        def _(it):
            copy_fresh_q(it).wait_recv()
            bring = load(chunk(stored_q.at[0], it), chunk(own_q, it), L_CHUNK)
            bring.start()
            bring.wait()
            forward_step(it, own_q, side_vm, 1, keys, values, mask, own_cot)
            load(chunk(own_cot, it), chunk(att_out.at[0], it), L_ATT).start()

        load(own_cot, att_out.at[0], L_ATT).wait()
        copy_gkv.wait_send()
        copy_gq.wait_send()
        copy_gain.wait_send()

    @pl.when(giver)
    def _():
        copy_side.wait_send()
        copy_gkv.wait_recv()
        copy_gq.wait_recv()
        copy_gain.wait_recv()

    @pl.when(jnp.logical_not(taker))
    def _():
        copy_cot.wait_send()
        copy_att.wait_recv()
        for copy in fresh_copies:
            copy.wait_send()
            copy.wait_recv()

    @pl.when(jnp.logical_not(giver))
    def _():
        copy_att.wait_send()
        put_gq.wait()
        put_gkv.wait()
        put_gain.wait()


def in_hbm(x):
    return pltpu.with_memory_space_constraint(x, pltpu.HBM)


def finish(*refs):
    half = len(refs) // 2
    copies = [pltpu.make_async_copy(refs[i], refs[half + i], refs[-1].at[i]) for i in range(half)]
    for copy in copies:
        copy.start()
    for copy in copies:
        copy.wait()


def local_tick(sections, replicas, fresh_q, fresh_kv, held_q, held_kv, cot, gains, plan, segment_ids):
    tokens, width, kv_width = fresh_q.shape[1], fresh_q.shape[2], fresh_kv.shape[2]
    ring = replicas // PLACES // CORES
    wide, narrow = (tokens, width), (tokens, kv_width)
    anywhere, hbm = pl.BlockSpec(memory_space=pl.ANY), pl.BlockSpec(memory_space=pltpu.HBM)
    shape = jax.ShapeDtypeStruct
    out_shape = (
        shape((1, *wide), BF16), shape((1, *wide), BF16), shape((1, *narrow), BF16),
        shape((1, *wide), BF16), shape((1, *narrow), BF16), shape((1, 2, D), F32),
    )
    outs = pl.pallas_call(
        functools.partial(kernel, sections, replicas),
        out_shape=out_shape,
        in_specs=[hbm] * 8,
        out_specs=(anywhere,) * 6,
        scratch_shapes=[
            pltpu.VMEM(wide, BF16), pltpu.VMEM(narrow, BF16), pltpu.VMEM(wide, BF16),
            pltpu.VMEM(wide, BF16), pltpu.VMEM(narrow, BF16), pltpu.VMEM(wide, BF16),
            pltpu.VMEM(wide, BF16), pltpu.VMEM(narrow, BF16), pltpu.VMEM((2, 8, D), F32),
            pltpu.VMEM(wide, BF16), pltpu.VMEM(narrow, BF16), pltpu.VMEM(wide, BF16),
            pltpu.VMEM(wide, BF16), pltpu.VMEM(narrow, BF16),
            pltpu.VMEM((KV_HEADS, D, D), BF16), pltpu.VMEM((KV_HEADS, D, D), BF16),
            pltpu.VMEM((tokens, D), F32),
            pltpu.VMEM((KV_HEADS, D, D), F32), pltpu.VMEM((KV_HEADS, D, D), F32),
            pltpu.VMEM((2, 8, D), F32),
            pltpu.VMEM((8, 2, 2, D), F32), pltpu.VMEM((ring, 2, 2, D), F32), pltpu.VMEM((2, 2, D), F32),
            pltpu.VMEM((2, D), F32), pltpu.VMEM(segment_ids.shape[1:], jnp.int32), pltpu.SMEM((1, 2), jnp.int32),
            pltpu.SemaphoreType.DMA((ROUND + ring + 3,)),
            pltpu.SemaphoreType.DMA((ROUND + ring + 3,)),
            pltpu.SemaphoreType.DMA((L_CHUNK + 1,)),
            pltpu.SemaphoreType.REGULAR,
        ],
        compiler_params=pltpu.CompilerParams(collective_id=0, has_side_effects=True, vmem_limit_bytes=VMEM_LIMIT),
    )(*(in_hbm(x) for x in (fresh_q, fresh_kv, held_q, held_kv, cot, gains, plan, segment_ids)))
    return pl.pallas_call(
        finish,
        out_shape=out_shape,
        in_specs=[anywhere] * 6,
        out_specs=(hbm,) * 6,
        scratch_shapes=[pltpu.SemaphoreType.DMA((6,))],
        compiler_params=pltpu.CompilerParams(vmem_limit_bytes=2**20),
    )(*outs)


VMEM_LIMIT = 16 * 2**20


def solution(mesh):
    tokens = P("section", "dp", None)
    return jax.shard_map(
        functools.partial(local_tick, mesh.shape["section"], mesh.shape["dp"]),
        mesh=mesh,
        in_specs=(tokens,) * 5 + (P("section", None, None), P("section", None), P("dp", None, None)),
        out_specs=(tokens,) * 5 + (P("section", None, None),),
        check_vma=False,
    )
```
